32 devices in a mesh: img: 8 (over z, y), gy: 4 (over x, core).
Axes of the slice: x: 2, y: 2, z: 4, core: 2. Of those that a mesh axis runs over, the one named last changes fastest.
Arguments:
- path: float32 [32, 4, 128, 128], P('img', None, 'gy'), may hold values from -1.2 to 1.2
- start_image: float32 [4, 128, 128], P(None, 'gy'), may hold values from -1.2 to 1.2
- end_image: float32 [4, 128, 128], P(None, 'gy'), may hold values from -1.2 to 1.2
- labels: int32 [4, 128, 128], P(None, 'gy'), may hold values from 0 to 3
- mob_table: float32 [4], replicated, may hold values from 0.2 to 2
Outputs:
- new_path: float32 [32, 4, 128, 128], P('img', None, 'gy')
The draws below stay inside these ranges and needn't reach their ends.
All inputs are finite; a program needn't handle non-finite values.
Results may differ from the reference program's by a relative error of at most 0.0001.
Values sent between devices are 32-bit elements; how exact they have to be, the bound alone decides.
No kernel may reach another device: no remote copies, remote signals or barrier semaphores. Data moves between devices by JAX's collectives and lax.ppermute only.
A program may use at most 64 MiB of HBM per device.

```python
import math
import jax
import jax.numpy as jnp
from jax import lax

X = 4
Z = 128
LEVELS = 4
ITERS = 2
IMAGES = 32
Y = 128


def set_ends(entries, key, smallest, high):
    extent = entries.shape
    place = [jax.random.randint(jax.random.fold_in(key, axis), (), 0, extent[axis]) for axis in range(len(extent))]
    entries = entries.at[tuple(place)].set(smallest)
    longest = extent.index(max(extent))
    place[longest] = (place[longest] + 1) % extent[longest]
    return entries.at[tuple(place)].set(high)


def levels(own_key, shape, split, least, high):
    level = 1.0
    for axis_at, blocks in split:
        draws = jax.random.uniform(jax.random.fold_in(jax.random.fold_in(own_key, 6), axis_at), (blocks,), jnp.float32, least / len(split), high / len(split))
        level = level * jnp.repeat(jnp.exp(draws), shape[axis_at] // blocks).reshape((-1,) + (1,) * (len(shape) - 1 - axis_at))
    return level


def setup_inputs(seed: int = 0) -> dict:
    key_of = jax.random.split(jax.random.key(seed), 6)
    return {
        "path": jnp.clip(jax.random.uniform(key_of[0], (IMAGES, X, Y, Z), jnp.float32, -1.2, 1.2) * levels(key_of[0], (IMAGES, X, Y, Z), ((0, 8), (2, 4)), -0.4, 0.0), -1.2, 1.2),
        "start_image": jnp.clip(jax.random.uniform(key_of[1], (X, Y, Z), jnp.float32, -1.2, 1.2) * levels(key_of[1], (X, Y, Z), ((1, 4),), -0.4, 0.0), -1.2, 1.2),
        "end_image": jnp.clip(jax.random.uniform(key_of[2], (X, Y, Z), jnp.float32, -1.2, 1.2) * levels(key_of[2], (X, Y, Z), ((1, 4),), -0.4, 0.0), -1.2, 1.2),
        "labels": set_ends(jax.random.randint(key_of[3], (X, Y, Z), 0, LEVELS), jax.random.fold_in(key_of[3], 1), 0, LEVELS - 1).astype(jnp.int32),
        "mob_table": jnp.clip(jnp.exp(jax.random.uniform(key_of[4], (LEVELS,), jnp.float32, math.log(0.2), math.log(2.0))), 0.2, 2.0),
    }


time_step = 0.5
stiffness = 0.25
step_length = 0.05

def mobility(labels, table):
    result = jnp.zeros(labels.shape, jnp.float32)
    for level in range(table.shape[0]):
        result = result + jnp.where(labels == level, table[level], jnp.float32(0.0))
    return result

def pad_y(field):
    widths = [(0, 0)] * (field.ndim - 2) + [(1, 1), (0, 0)]
    return jnp.pad(field, widths)

def laplace(padded):
    centre = padded[..., 1:-1, :]
    total = jnp.roll(centre, 1, -3) + jnp.roll(centre, -1, -3)
    total = total + jnp.roll(centre, 1, -1) + jnp.roll(centre, -1, -1)
    return total + padded[..., 2:, :] + padded[..., :-2, :] - 6.0 * centre

def drift(padded, mob):
    centre = padded[..., 1:-1, :]
    return mob * (stiffness * laplace(padded) + centre - centre * centre * centre)

def reference(path, start_image, end_image, labels, mob_table):
    mob = mobility(labels, mob_table)
    count = path.shape[0]
    weights = jnp.arange(1, count + 1).astype(jnp.float32)[:, None, None, None]
    for step in range(ITERS):
        full = jnp.concatenate([start_image[None], path, end_image[None]], 0)
        force = drift(pad_y(full[:-1]), mob)
        resid = (full[1:] - full[:-1]) / time_step - force
        mres = mob * resid[1:]
        adjoint = stiffness * laplace(pad_y(mres)) + (1.0 - 3.0 * path * path) * mres
        grad = (resid[:-1] - resid[1:]) / time_step - adjoint
        weighted = weights * grad
        before_g = jnp.cumsum(grad, 0) - grad
        before_q = jnp.cumsum(weighted, 0) - weighted
        coeff = lax.optimization_barrier(jnp.sum(grad, 0)) - lax.optimization_barrier(jnp.sum(weighted, 0)) / (count + 1)
        update = time_step * time_step * (weights * coeff - weights * before_g + before_q)
        scale = step_length / jnp.sqrt(jnp.mean(update * update) + 1e-06)
        path = path - scale * update
    return path
```

```python
import functools

import jax
import jax.numpy as jnp
from jax import lax
from jax.experimental import pallas as pl
from jax.experimental.pallas import tpu as pltpu
from jax.sharding import PartitionSpec as P

ITERS = 2


time_step = 0.5
stiffness = 0.25
step_length = 0.05


def extended_2(shard, sides, width):
    for axis, dim in sides:
        size, length = (lax.axis_size(axis), shard.shape[dim])
        up = [(i, (i + 1) % size) for i in range(size - 1)]
        down = [(j, i) for i, j in up]
        last = lax.slice_in_dim(shard, length - width, length, axis=dim)
        initial = lax.slice_in_dim(shard, 0, width, axis=dim)
        before = lax.ppermute(last, axis, up)
        after = lax.ppermute(initial, axis, down)
        shard = jnp.concatenate([before, shard, after], axis=dim)
    return shard


def shifted(block, axis, distance):
    devices = range(lax.axis_size(axis))
    route = [(i - distance, i) for i in devices if i - distance in devices]
    return lax.ppermute(block, axis, route)


def mobility(labels, table):
    result = jnp.zeros(labels.shape, jnp.float32)
    for level in range(table.shape[0]):
        result = result + jnp.where(labels == level, table[level], jnp.float32(0.0))
    return result


def laplace(padded):
    centre = padded[..., 1:-1, :]
    total = jnp.roll(centre, 1, -3) + jnp.roll(centre, -1, -3)
    total = total + jnp.roll(centre, 1, -1) + jnp.roll(centre, -1, -1)
    return total + padded[..., 2:, :] + padded[..., :-2, :] - 6.0 * centre


def drift(padded, mob):
    centre = padded[..., 1:-1, :]
    return mob * (stiffness * laplace(padded) + centre - centre * centre * centre)


def general(path, start_image, end_image, labels, mob_table):
    count = path.shape[0]
    groups = lax.axis_size("img")
    images = count * groups
    rank = lax.axis_index("img")
    is_first = rank == 0
    is_final = rank == groups - 1
    gy_count = lax.axis_size("gy")
    rows_here = path.shape[2]
    cells = images * path.shape[1] * rows_here * gy_count * path.shape[3]
    mob = mobility(labels, mob_table)
    for step in range(ITERS):
        extended = jnp.concatenate([start_image[None], path], 0)
        padded = extended_2(extended, (("gy", 2),), 1)
        force = drift(padded, mob)
        current = padded[1 : count + 1, :, 1:-1, :]
        start_part = padded[0, :, 1:-1, :]
        ahead = shifted(current[0], "img", -1)
        ahead = jnp.where(is_final, end_image, ahead)
        later = jnp.concatenate([current[1:], ahead[None]], 0)
        wide_res = (later - current) / time_step - force[1:]
        opening = (current[0] - start_part) / time_step - force[0]
        mres = mob * wide_res
        mpad = extended_2(mres, (("gy", 2),), 1)
        previous = shifted(wide_res[-1], "img", 1)
        previous = jnp.where(is_first, opening, previous)
        earlier = jnp.concatenate([previous[None], wide_res[:-1]], 0)
        adjoint = stiffness * laplace(mpad) + (1.0 - 3.0 * path * path) * mres
        grad = (earlier - wide_res) / time_step - adjoint
        flat = grad.reshape(count, groups, -1)
        columns = lax.all_to_all(flat, "img", split_axis=1, concat_axis=0, tiled=True)
        every = columns.shape[0]
        index = jnp.arange(1, every + 1).astype(jnp.float32)[:, None, None]
        scaled = index * columns
        before_g = jnp.cumsum(columns, 0) - columns
        before_q = jnp.cumsum(scaled, 0) - scaled
        coeff = jnp.sum(columns, 0) - jnp.sum(scaled, 0) / (every + 1)
        solved = time_step * time_step * (index * coeff[None] - index * before_g + before_q)
        back = lax.all_to_all(solved, "img", split_axis=0, concat_axis=1, tiled=True)
        update = back.reshape(grad.shape)
        squares = lax.psum(jnp.sum(update * update), ("img", "gy"))
        scale = step_length * lax.rsqrt(squares / cells + 1e-06)
        path = path - scale * update
    return path


def walk(mesh):
    count = mesh.shape["img"]
    plain = list(range(count))
    try:
        line = mesh.devices.reshape(count, -1)[:, 0]
        place = [tuple(d.coords) for d in line]
    except Exception:
        return plain

    def near(a, b):
        return sum(abs(p - q) for p, q in zip(place[a], place[b])) <= 1

    def grow(order):
        if len(order) == count:
            return order
        for nxt in plain:
            if nxt not in order and near(order[-1], nxt):
                found = grow(order + [nxt])
                if found:
                    return found
        return None

    return grow([0]) or plain


def spread(order, position, flip):
    return jnp.where(flip == 1, order[len(order) - 1 - position], order[position])


def pack_kernel(order, path_ref, start_ref, end_ref, labels_ref, table_ref, out_ref):
    images, planes, rows, lanes = path_ref.shape
    groups = len(order)
    flip = lax.rem(lax.axis_index("gy"), 2)
    rank = lax.axis_index("img")
    slab = rank // 2
    odd = lax.rem(rank, 2) == 1
    for c in range(groups):
        dest = spread(order, c, flip)
        for m in range(images):
            for h in range(2):
                row = 4 * c + 2 * h
                parts = [path_ref[m, x, row : row + 2, :] for x in range(planes)]
                out_ref[dest, 2 * m + h] = jnp.concatenate(parts, 0)
        extra = []
        for h in range(2):
            row = 4 * c + 2 * h

            def tile(ref):
                parts = [ref[x, row : row + 2, :] for x in range(planes)]
                return jnp.concatenate(parts, 0)

            label = tile(labels_ref)
            mob = jnp.zeros(label.shape, jnp.float32)
            for level in range(table_ref.shape[0]):
                mob = mob + jnp.where(label == level, table_ref[level], jnp.float32(0.0))
            ends = jnp.where(slab == 0, tile(start_ref), tile(end_ref))
            extra.append(jnp.where(slab >= 2, mob, ends))
        out_ref[dest, 2 * images] = jnp.where(odd, extra[1], extra[0])


def lap(tiles, first, r_is_0):
    out = []
    pair = [tiles[h] + tiles[h + 1] for h in range(len(tiles) - 1)]
    for h in range(1, len(tiles) - 1):
        v = tiles[h]
        total = pltpu.roll(v, 2, 0) + pltpu.roll(v, 6, 0)
        total = total + pltpu.roll(v, 1, 1) + pltpu.roll(v, 127, 1)
        y = jnp.where(r_is_0, pltpu.roll(pair[h - 1], 7, 0), pltpu.roll(pair[h], 1, 0))
        out.append(total + y - 6.0 * v)
    return out


def pad_zero(tiles):
    zero = jnp.zeros_like(tiles[0])
    return [zero] + list(tiles) + [zero]


def residual(now, ahead, mob, r_is_0):
    bend = lap(pad_zero(now), 0, r_is_0)
    out = []
    for v, w, q, m in zip(now, ahead, bend, mob):
        force = m * (stiffness * q + v - v * v * v)
        out.append((w - v) * (1.0 / time_step) - force)
    return out


def gradient(now, before, resid, mob, r_is_0):
    mres = [m * r for m, r in zip(mob, resid)]
    bend = lap(mres, 0, r_is_0)
    out = []
    for n, q in enumerate(bend):
        v = now[n + 1]
        adjoint = stiffness * q + (1.0 - 3.0 * v * v) * mres[n + 1]
        out.append((before[n] - resid[n + 1]) * (1.0 / time_step) - adjoint)
    return out


def row_parity(shape):
    return lax.rem(lax.broadcasted_iota(jnp.int32, shape, 0), 2) == 0


def fetch(refs, group, tile_at):
    out = []
    for ref in refs:
        out += [ref[group, tile_at], ref[group, tile_at + 1]]
    return out


def fetch_extra(refs, slab):
    last = refs[0].shape[1] - 1
    out = []
    for ref in refs:
        out += [ref[2 * slab, last], ref[2 * slab + 1, last]]
    return out


def first_kernel(own_ref, prev_ref, next_ref, w_ref, part_ref):
    refs = (prev_ref, own_ref, next_ref)
    groups, per = own_ref.shape[0], own_ref.shape[1] // 2
    count = groups * per
    shape = own_ref.shape[2:]
    even = row_parity(shape)
    mob = fetch_extra(refs, 2)
    start = fetch_extra(refs, 0)
    now = fetch(refs, 0, 0)
    r0 = residual(start, now, mob, even)
    zero = jnp.zeros(shape, jnp.float32)
    carry = tuple(r0[1:-1]), (zero,) * 4, (zero,) * 4

    def group_step(i, carry, last_group):
        before, psum, w = carry
        for m in range(per):
            now = fetch(refs, i, 2 * m)
            if m < per - 1:
                ahead = fetch(refs, i, 2 * m + 2)
            elif last_group:
                ahead = fetch_extra(refs, 1)
            else:
                ahead = fetch(refs, i + 1, 0)
            mob_now = fetch_extra(refs, 2)
            resid = residual(now, ahead, mob_now, even)
            grad = gradient(now, before, resid, mob_now, even)
            for t in range(4):
                w_ref[i * per + m, t] = w[t]
            psum = tuple(p + g for p, g in zip(psum, grad))
            w = tuple(a - p for a, p in zip(w, psum))
            before = tuple(resid[1:-1])
        return before, psum, w

    carry = lax.fori_loop(
        0, groups - 1, lambda i, c: group_step(i, c, False), carry
    )
    _, _, w = group_step(groups - 1, carry, True)
    for t in range(4):
        w_ref[count, t] = w[t]
    share = [w[t] * (1.0 / (count + 1)) for t in (1, 2)]

    def square_step(i, total):
        for m in range(per):
            k = i * per + m
            at = (k + 1).astype(jnp.float32)
            for n, t in enumerate((1, 2)):
                u = time_step * time_step * (w_ref[k, t] - at * share[n])
                total = total + u * u
        return total

    total = lax.fori_loop(0, groups, square_step, zero)
    line = jnp.sum(total, axis=0, keepdims=True)
    part_ref[...] = jnp.broadcast_to(line, part_ref.shape)


def second_kernel(cells, order, own_ref, prev_ref, next_ref, w_ref, parts_ref, out_ref, part_ref):
    refs = (prev_ref, own_ref, next_ref)
    groups, per = own_ref.shape[0], own_ref.shape[1] // 2
    count = groups * per
    shape = own_ref.shape[2:]
    even = row_parity(shape)
    scale = step_length * lax.rsqrt(jnp.sum(parts_ref[...]) / cells + 1e-06)
    scale = scale * (time_step * time_step)
    gy, rank = lax.axis_index("gy"), lax.axis_index("img")
    flip = lax.rem(gy, 2)
    opens = (gy == 0) & (rank == order[0])
    final = lax.axis_size("gy") - 1
    last_rank = order[0] if final % 2 else order[-1]
    closes = (gy == final) & (rank == last_rank)
    none = jnp.float32(0.0)
    scales = [jnp.where(opens, none, scale), scale, scale, jnp.where(closes, none, scale)]
    share = [w_ref[count, t] * (1.0 / (count + 1)) for t in range(4)]

    def moved(i, m):
        k = i * per + m
        at = jnp.asarray(k + 1, jnp.int32).astype(jnp.float32)
        tiles = fetch(refs, i, 2 * m)[1:-1]
        return [v - s * (w_ref[k, t] - at * c) for t, (v, s, c) in enumerate(zip(tiles, scales, share))]

    mob = fetch_extra(refs, 2)[1:-1]
    start = fetch_extra(refs, 0)[1:-1]
    now = moved(0, 0)
    r0 = residual(start, now, mob, even)
    zero = jnp.zeros(shape, jnp.float32)
    carry = tuple(now), tuple(r0[1:-1]), (zero,) * 2, (zero,) * 2

    def group_step(i, carry, last_group):
        now, before, psum, w = carry
        for m in range(per):
            if m < per - 1:
                ahead = moved(i, m + 1)
            elif last_group:
                ahead = fetch_extra(refs, 1)[1:-1]
            else:
                ahead = moved(i + 1, 0)
            resid = residual(now, ahead, mob, even)
            grad = gradient(now, before, resid, mob, even)
            for t in range(2):
                out_ref[i, 4 * m + t] = now[t + 1]
                out_ref[i, 4 * m + 2 + t] = w[t]
            psum = tuple(p + g for p, g in zip(psum, grad))
            w = tuple(a - p for a, p in zip(w, psum))
            before = tuple(resid[1:-1])
            now = tuple(ahead)
        return now, before, psum, w

    carry = lax.fori_loop(
        0, groups - 1, lambda i, c: group_step(i, c, False), carry
    )
    w = group_step(groups - 1, carry, True)[3]
    share = [v * (1.0 / (count + 1)) for v in w]

    def square_step(i, total):
        for m in range(per):
            at = (i * per + m + 1).astype(jnp.float32)
            for t in range(2):
                u = time_step * time_step * (out_ref[i, 4 * m + 2 + t] - at * share[t])
                out_ref[i, 4 * m + 2 + t] = u
                total = total + u * u
        return total

    total = lax.fori_loop(0, groups, square_step, zero)
    line = jnp.sum(total, axis=0, keepdims=True)
    part_ref[...] = jnp.broadcast_to(line, part_ref.shape)


def unpack_kernel(cells, order, data_ref, parts_ref, out_ref):
    images, planes, rows, lanes = out_ref.shape
    groups = len(order)
    scale = step_length * lax.rsqrt(jnp.sum(parts_ref[...]) / cells + 1e-06)
    flip = lax.rem(lax.axis_index("gy"), 2)
    for c in range(groups):
        src = spread(order, c, flip)
        for m in range(images):
            for h in range(2):
                row = 4 * c + 2 * h
                v = data_ref[src, 4 * m + h] - scale * data_ref[src, 4 * m + 2 + h]
                for x in range(planes):
                    out_ref[m, x, row : row + 2, :] = v[2 * x : 2 * x + 2, :]


def call(kernel, outs, smem_at=None, count=0):
    specs = [pl.BlockSpec(memory_space=pltpu.VMEM) for _ in range(count)]
    if smem_at is not None:
        specs[smem_at] = pl.BlockSpec(memory_space=pltpu.SMEM)
    shapes = [jax.ShapeDtypeStruct(s, jnp.float32) for s in outs]
    out_specs = [pl.BlockSpec(memory_space=pltpu.VMEM) for _ in outs]
    if len(outs) == 1:
        shapes, out_specs = shapes[0], out_specs[0]
    return pl.pallas_call(kernel, out_shape=shapes, in_specs=specs, out_specs=out_specs)


def blocked(order, path, start_image, end_image, labels, mob_table):
    images, planes, rows, lanes = path.shape
    groups, slabs = lax.axis_size("img"), lax.axis_size("gy")
    both = ("img", "gy")
    every = groups * slabs
    tile = (2 * planes, lanes)
    cells = images * groups * planes * rows * slabs * lanes
    line = []
    for g in range(slabs):
        line += [i * slabs + g for i in (order[::-1] if g % 2 else order)]
    ahead = [(line[n], line[n + 1]) for n in range(every - 1)]
    back = [(b, a) for a, b in ahead]

    def swap(v, axis):
        return lax.all_to_all(v, axis, split_axis=0, concat_axis=0, tiled=True)

    packed = call(
        functools.partial(pack_kernel, order), [(groups, 2 * images + 1) + tile], 4, 5
    )(path, start_image, end_image, labels, mob_table)
    own = swap(packed, "img")
    prev = lax.ppermute(own, both, ahead)
    after = lax.ppermute(own, both, back)
    w, part = call(
        first_kernel, [(images * groups + 1, 4) + tile, (every, lanes)], None, 3
    )(own, prev, after)
    parts = swap(part, both)
    moved, part = call(
        functools.partial(second_kernel, cells, order),
        [(groups, 4 * images) + tile, (every, lanes)],
        None,
        5,
    )(own, prev, after, w, parts)
    parts = swap(part, both)
    home = swap(moved, "img")
    return call(functools.partial(unpack_kernel, cells, order), [path.shape], None, 2)(home, parts)


def solution(mesh):
    order = walk(mesh)

    def per_device(path, start_image, end_image, labels, mob_table):
        images, planes, rows, lanes = path.shape
        groups = lax.axis_size("img")
        fits = rows == 4 * groups and planes == 4 and lanes == 128 and groups >= 6
        if fits and ITERS == 2:
            return blocked(order, path, start_image, end_image, labels, mob_table)
        return general(path, start_image, end_image, labels, mob_table)

    in_specs = (
        P("img", None, "gy", None),
        P(None, "gy", None),
        P(None, "gy", None),
        P(None, "gy", None),
        P(),
    )
    out_specs = P("img", None, "gy", None)
    return jax.shard_map(
        per_device, mesh=mesh, in_specs=in_specs, out_specs=out_specs, check_vma=False
    )
```

```python
import functools

import jax
import jax.numpy as jnp
from jax import lax
from jax.experimental import pallas as pl
from jax.experimental.pallas import tpu as pltpu
from jax.sharding import PartitionSpec as P

ITERS = 2


time_step = 0.5
stiffness = 0.25
step_length = 0.05


def extended_2(shard, sides, width):
    for axis, dim in sides:
        size, length = (lax.axis_size(axis), shard.shape[dim])
        up = [(i, (i + 1) % size) for i in range(size - 1)]
        down = [(j, i) for i, j in up]
        last = lax.slice_in_dim(shard, length - width, length, axis=dim)
        initial = lax.slice_in_dim(shard, 0, width, axis=dim)
        before = lax.ppermute(last, axis, up)
        after = lax.ppermute(initial, axis, down)
        shard = jnp.concatenate([before, shard, after], axis=dim)
    return shard


def shifted(block, axis, distance):
    devices = range(lax.axis_size(axis))
    route = [(i - distance, i) for i in devices if i - distance in devices]
    return lax.ppermute(block, axis, route)


def mobility(labels, table):
    result = jnp.zeros(labels.shape, jnp.float32)
    for level in range(table.shape[0]):
        result = result + jnp.where(labels == level, table[level], jnp.float32(0.0))
    return result


def laplace(padded):
    centre = padded[..., 1:-1, :]
    total = jnp.roll(centre, 1, -3) + jnp.roll(centre, -1, -3)
    total = total + jnp.roll(centre, 1, -1) + jnp.roll(centre, -1, -1)
    return total + padded[..., 2:, :] + padded[..., :-2, :] - 6.0 * centre


def drift(padded, mob):
    centre = padded[..., 1:-1, :]
    return mob * (stiffness * laplace(padded) + centre - centre * centre * centre)


def general(path, start_image, end_image, labels, mob_table):
    count = path.shape[0]
    groups = lax.axis_size("img")
    images = count * groups
    rank = lax.axis_index("img")
    is_first = rank == 0
    is_final = rank == groups - 1
    gy_count = lax.axis_size("gy")
    rows_here = path.shape[2]
    cells = images * path.shape[1] * rows_here * gy_count * path.shape[3]
    mob = mobility(labels, mob_table)
    for step in range(ITERS):
        extended = jnp.concatenate([start_image[None], path], 0)
        padded = extended_2(extended, (("gy", 2),), 1)
        force = drift(padded, mob)
        current = padded[1 : count + 1, :, 1:-1, :]
        start_part = padded[0, :, 1:-1, :]
        ahead = shifted(current[0], "img", -1)
        ahead = jnp.where(is_final, end_image, ahead)
        later = jnp.concatenate([current[1:], ahead[None]], 0)
        wide_res = (later - current) / time_step - force[1:]
        opening = (current[0] - start_part) / time_step - force[0]
        mres = mob * wide_res
        mpad = extended_2(mres, (("gy", 2),), 1)
        previous = shifted(wide_res[-1], "img", 1)
        previous = jnp.where(is_first, opening, previous)
        earlier = jnp.concatenate([previous[None], wide_res[:-1]], 0)
        adjoint = stiffness * laplace(mpad) + (1.0 - 3.0 * path * path) * mres
        grad = (earlier - wide_res) / time_step - adjoint
        flat = grad.reshape(count, groups, -1)
        columns = lax.all_to_all(flat, "img", split_axis=1, concat_axis=0, tiled=True)
        every = columns.shape[0]
        index = jnp.arange(1, every + 1).astype(jnp.float32)[:, None, None]
        scaled = index * columns
        before_g = jnp.cumsum(columns, 0) - columns
        before_q = jnp.cumsum(scaled, 0) - scaled
        coeff = jnp.sum(columns, 0) - jnp.sum(scaled, 0) / (every + 1)
        solved = time_step * time_step * (index * coeff[None] - index * before_g + before_q)
        back = lax.all_to_all(solved, "img", split_axis=0, concat_axis=1, tiled=True)
        update = back.reshape(grad.shape)
        squares = lax.psum(jnp.sum(update * update), ("img", "gy"))
        scale = step_length * lax.rsqrt(squares / cells + 1e-06)
        path = path - scale * update
    return path


def walk(mesh):
    count = mesh.shape["img"]
    plain = list(range(count))
    try:
        line = mesh.devices.reshape(count, -1)[:, 0]
        place = [tuple(d.coords) for d in line]
    except Exception:
        return plain

    def near(a, b):
        return sum(abs(p - q) for p, q in zip(place[a], place[b])) <= 1

    def grow(order):
        if len(order) == count:
            return order
        for nxt in plain:
            if nxt not in order and near(order[-1], nxt):
                found = grow(order + [nxt])
                if found:
                    return found
        return None

    return grow([0]) or plain


def spread(order, position, flip):
    return jnp.where(flip == 1, order[len(order) - 1 - position], order[position])


def pack_kernel(order, path_ref, start_ref, end_ref, labels_ref, table_ref, out_ref):
    images, planes, rows, lanes = path_ref.shape
    groups = len(order)
    flip = lax.rem(lax.axis_index("gy"), 2)
    rank = lax.axis_index("img")
    slab = rank // 2
    odd = lax.rem(rank, 2) == 1
    for c in range(groups):
        dest = spread(order, c, flip)
        for m in range(images):
            for h in range(2):
                row = 4 * c + 2 * h
                parts = [path_ref[m, x, row : row + 2, :] for x in range(planes)]
                out_ref[dest, 2 * m + h] = jnp.concatenate(parts, 0)
        extra = []
        for h in range(2):
            row = 4 * c + 2 * h

            def tile(ref):
                parts = [ref[x, row : row + 2, :] for x in range(planes)]
                return jnp.concatenate(parts, 0)

            label = tile(labels_ref)
            mob = jnp.zeros(label.shape, jnp.float32)
            for level in range(table_ref.shape[0]):
                mob = mob + jnp.where(label == level, table_ref[level], jnp.float32(0.0))
            ends = jnp.where(slab == 0, tile(start_ref), tile(end_ref))
            extra.append(jnp.where(slab >= 2, mob, ends))
        out_ref[dest, 2 * images] = jnp.where(odd, extra[1], extra[0])


def lap(tiles, first, r_is_0):
    out = []
    pair = [tiles[h] + tiles[h + 1] for h in range(len(tiles) - 1)]
    for h in range(1, len(tiles) - 1):
        v = tiles[h]
        total = pltpu.roll(v, 2, 0) + pltpu.roll(v, 6, 0)
        total = total + pltpu.roll(v, 1, 1) + pltpu.roll(v, 127, 1)
        y = jnp.where(r_is_0, pltpu.roll(pair[h - 1], 7, 0), pltpu.roll(pair[h], 1, 0))
        out.append(total + y - 6.0 * v)
    return out


def pad_zero(tiles):
    zero = jnp.zeros_like(tiles[0])
    return [zero] + list(tiles) + [zero]


def residual(now, ahead, mob, r_is_0):
    bend = lap(pad_zero(now), 0, r_is_0)
    out = []
    for v, w, q, m in zip(now, ahead, bend, mob):
        force = m * (stiffness * q + v - v * v * v)
        out.append((w - v) * (1.0 / time_step) - force)
    return out


def gradient(now, before, resid, mob, r_is_0):
    mres = [m * r for m, r in zip(mob, resid)]
    bend = lap(mres, 0, r_is_0)
    out = []
    for n, q in enumerate(bend):
        v = now[n + 1]
        adjoint = stiffness * q + (1.0 - 3.0 * v * v) * mres[n + 1]
        out.append((before[n] - resid[n + 1]) * (1.0 / time_step) - adjoint)
    return out


def row_parity(shape):
    return lax.rem(lax.broadcasted_iota(jnp.int32, shape, 0), 2) == 0


def fetch(refs, group, tile_at):
    out = []
    for ref in refs:
        out += [ref[group, tile_at], ref[group, tile_at + 1]]
    return out


def fetch_extra(refs, slab):
    last = refs[0].shape[1] - 1
    out = []
    for ref in refs:
        out += [ref[2 * slab, last], ref[2 * slab + 1, last]]
    return out


def first_kernel(own_ref, prev_ref, next_ref, w_ref, part_ref):
    refs = (prev_ref, own_ref, next_ref)
    groups, per = own_ref.shape[0], own_ref.shape[1] // 2
    count = groups * per
    shape = own_ref.shape[2:]
    even = row_parity(shape)
    mob = fetch_extra(refs, 2)
    start = fetch_extra(refs, 0)
    now = fetch(refs, 0, 0)
    r0 = residual(start, now, mob, even)
    zero = jnp.zeros(shape, jnp.float32)
    carry = tuple(r0[1:-1]), (zero,) * 4, (zero,) * 4

    def group_step(i, carry, last_group):
        before, psum, w = carry
        for m in range(per):
            now = fetch(refs, i, 2 * m)
            if m < per - 1:
                ahead = fetch(refs, i, 2 * m + 2)
            elif last_group:
                ahead = fetch_extra(refs, 1)
            else:
                ahead = fetch(refs, i + 1, 0)
            mob_now = fetch_extra(refs, 2)
            resid = residual(now, ahead, mob_now, even)
            grad = gradient(now, before, resid, mob_now, even)
            for t in range(4):
                w_ref[i * per + m, t] = w[t]
            psum = tuple(p + g for p, g in zip(psum, grad))
            w = tuple(a - p for a, p in zip(w, psum))
            before = tuple(resid[1:-1])
        return before, psum, w

    carry = lax.fori_loop(
        0, groups - 1, lambda i, c: group_step(i, c, False), carry
    )
    _, _, w = group_step(groups - 1, carry, True)
    for t in range(4):
        w_ref[count, t] = w[t]
    share = [w[t] * (1.0 / (count + 1)) for t in (1, 2)]

    def square_step(i, total):
        for m in range(per):
            k = i * per + m
            at = (k + 1).astype(jnp.float32)
            for n, t in enumerate((1, 2)):
                u = time_step * time_step * (w_ref[k, t] - at * share[n])
                total = total + u * u
        return total

    total = lax.fori_loop(0, groups, square_step, zero)
    line = jnp.sum(total, axis=0, keepdims=True)
    part_ref[...] = jnp.broadcast_to(line, part_ref.shape)


def second_kernel(cells, order, own_ref, prev_ref, next_ref, w_ref, parts_ref, out_ref, part_ref):
    refs = (prev_ref, own_ref, next_ref)
    groups, per = own_ref.shape[0], own_ref.shape[1] // 2
    count = groups * per
    shape = own_ref.shape[2:]
    even = row_parity(shape)
    scale = step_length * lax.rsqrt(jnp.sum(parts_ref[...]) / cells + 1e-06)
    scale = scale * (time_step * time_step)
    gy, rank = lax.axis_index("gy"), lax.axis_index("img")
    flip = lax.rem(gy, 2)
    opens = (gy == 0) & (rank == order[0])
    final = lax.axis_size("gy") - 1
    last_rank = order[0] if final % 2 else order[-1]
    closes = (gy == final) & (rank == last_rank)
    none = jnp.float32(0.0)
    scales = [jnp.where(opens, none, scale), scale, scale, jnp.where(closes, none, scale)]
    share = [w_ref[count, t] * (1.0 / (count + 1)) for t in range(4)]

    def moved(i, m):
        k = i * per + m
        at = jnp.asarray(k + 1, jnp.int32).astype(jnp.float32)
        tiles = fetch(refs, i, 2 * m)[1:-1]
        return [v - s * (w_ref[k, t] - at * c) for t, (v, s, c) in enumerate(zip(tiles, scales, share))]

    mob = fetch_extra(refs, 2)[1:-1]
    start = fetch_extra(refs, 0)[1:-1]
    now = moved(0, 0)
    r0 = residual(start, now, mob, even)
    zero = jnp.zeros(shape, jnp.float32)
    carry = tuple(now), tuple(r0[1:-1]), (zero,) * 2, (zero,) * 2

    def group_step(i, carry, last_group):
        now, before, psum, w = carry
        for m in range(per):
            if m < per - 1:
                ahead = moved(i, m + 1)
            elif last_group:
                ahead = fetch_extra(refs, 1)[1:-1]
            else:
                ahead = moved(i + 1, 0)
            resid = residual(now, ahead, mob, even)
            grad = gradient(now, before, resid, mob, even)
            for t in range(2):
                out_ref[i, 4 * m + t] = now[t + 1]
                out_ref[i, 4 * m + 2 + t] = w[t]
            psum = tuple(p + g for p, g in zip(psum, grad))
            w = tuple(a - p for a, p in zip(w, psum))
            before = tuple(resid[1:-1])
            now = tuple(ahead)
        return now, before, psum, w

    carry = lax.fori_loop(
        0, groups - 1, lambda i, c: group_step(i, c, False), carry
    )
    w = group_step(groups - 1, carry, True)[3]
    share = [v * (1.0 / (count + 1)) for v in w]

    def square_step(i, total):
        for m in range(per):
            at = (i * per + m + 1).astype(jnp.float32)
            for t in range(2):
                u = time_step * time_step * (out_ref[i, 4 * m + 2 + t] - at * share[t])
                out_ref[i, 4 * m + 2 + t] = u
                total = total + u * u
        return total

    total = lax.fori_loop(0, groups, square_step, zero)
    line = jnp.sum(total, axis=0, keepdims=True)
    part_ref[...] = jnp.broadcast_to(line, part_ref.shape)


def last_kernel(cells, data_ref, parts_ref, out_ref):
    groups, per = out_ref.shape[0], out_ref.shape[1] // 2
    scale = step_length * lax.rsqrt(jnp.sum(parts_ref[...]) / cells + 1e-06)
    for i in range(groups):
        for m in range(per):
            for t in range(2):
                out_ref[i, 2 * m + t] = data_ref[i, 4 * m + t] - scale * data_ref[i, 4 * m + 2 + t]


def unpack_kernel(order, data_ref, out_ref):
    images, planes, rows, lanes = out_ref.shape
    groups = len(order)
    flip = lax.rem(lax.axis_index("gy"), 2)
    for c in range(groups):
        src = spread(order, c, flip)
        for m in range(images):
            for h in range(2):
                row = 4 * c + 2 * h
                v = data_ref[src, 2 * m + h]
                for x in range(planes):
                    out_ref[m, x, row : row + 2, :] = v[2 * x : 2 * x + 2, :]


VMEM_LIMIT = 16 * 1024 * 1024
WHOLE_VMEM = 67043328


def call(kernel, outs, count, scalars=0, limit=VMEM_LIMIT):
    shapes = [jax.ShapeDtypeStruct(s, jnp.float32) for s in outs]
    places = [pl.BlockSpec(memory_space=pltpu.VMEM) for _ in outs]
    single = len(outs) == 1
    return pl.pallas_call(
        kernel,
        out_shape=shapes[0] if single else shapes,
        in_specs=[pl.BlockSpec(memory_space=pltpu.VMEM)] * count
        + [pl.BlockSpec(memory_space=pltpu.SMEM)] * scalars,
        out_specs=places[0] if single else places,
        compiler_params=pltpu.CompilerParams(vmem_limit_bytes=limit),
    )


def blocked(order, path, start_image, end_image, labels, mob_table):
    images, planes, rows, lanes = path.shape
    groups, slabs = lax.axis_size("img"), lax.axis_size("gy")
    both = ("img", "gy")
    every = groups * slabs
    tile = (2 * planes, lanes)
    cells = images * groups * planes * rows * slabs * lanes
    line = []
    for g in range(slabs):
        line += [i * slabs + g for i in (order[::-1] if g % 2 else order)]
    ahead = [(line[n], line[n + 1]) for n in range(every - 1)]
    back = [(b, a) for a, b in ahead]

    def swap(v, axis):
        return lax.all_to_all(v, axis, split_axis=0, concat_axis=0, tiled=True)

    packed = call(
        functools.partial(pack_kernel, order),
        [(groups, 2 * images + 1) + tile],
        4,
        scalars=1,
        limit=WHOLE_VMEM,
    )(path, start_image, end_image, labels, mob_table)
    own = swap(packed, "img")
    prev = lax.ppermute(own, both, ahead)
    after = lax.ppermute(own, both, back)
    w, part = call(first_kernel, [(images * groups + 1, 4) + tile, (every, lanes)], 3)(
        own, prev, after
    )
    parts = swap(part, both)
    moved, part = call(
        functools.partial(second_kernel, cells, order),
        [(groups, 4 * images) + tile, (every, lanes)],
        5,
    )(own, prev, after, w, parts)
    parts = swap(part, both)
    done = call(functools.partial(last_kernel, cells), [(groups, 2 * images) + tile], 2)(
        moved, parts
    )
    home = swap(done, "img")
    return call(functools.partial(unpack_kernel, order), [path.shape], 1)(home)


def solution(mesh):
    order = walk(mesh)

    def per_device(path, start_image, end_image, labels, mob_table):
        images, planes, rows, lanes = path.shape
        groups = lax.axis_size("img")
        fits = rows == 4 * groups and planes == 4 and lanes == 128 and groups >= 6
        if fits and ITERS == 2:
            return blocked(order, path, start_image, end_image, labels, mob_table)
        return general(path, start_image, end_image, labels, mob_table)

    in_specs = (
        P("img", None, "gy", None),
        P(None, "gy", None),
        P(None, "gy", None),
        P(None, "gy", None),
        P(),
    )
    out_specs = P("img", None, "gy", None)
    return jax.shard_map(
        per_device, mesh=mesh, in_specs=in_specs, out_specs=out_specs, check_vma=False
    )
```

```python
import functools

import jax
import jax.numpy as jnp
from jax import lax
from jax.experimental import pallas as pl
from jax.experimental.pallas import tpu as pltpu
from jax.sharding import PartitionSpec as P

ITERS = 2


time_step = 0.5
stiffness = 0.25
step_length = 0.05


def extended_2(shard, sides, width):
    for axis, dim in sides:
        size, length = (lax.axis_size(axis), shard.shape[dim])
        up = [(i, (i + 1) % size) for i in range(size - 1)]
        down = [(j, i) for i, j in up]
        last = lax.slice_in_dim(shard, length - width, length, axis=dim)
        initial = lax.slice_in_dim(shard, 0, width, axis=dim)
        before = lax.ppermute(last, axis, up)
        after = lax.ppermute(initial, axis, down)
        shard = jnp.concatenate([before, shard, after], axis=dim)
    return shard


def shifted(block, axis, distance):
    devices = range(lax.axis_size(axis))
    route = [(i - distance, i) for i in devices if i - distance in devices]
    return lax.ppermute(block, axis, route)


def mobility(labels, table):
    result = jnp.zeros(labels.shape, jnp.float32)
    for level in range(table.shape[0]):
        result = result + jnp.where(labels == level, table[level], jnp.float32(0.0))
    return result


def laplace(padded):
    centre = padded[..., 1:-1, :]
    total = jnp.roll(centre, 1, -3) + jnp.roll(centre, -1, -3)
    total = total + jnp.roll(centre, 1, -1) + jnp.roll(centre, -1, -1)
    return total + padded[..., 2:, :] + padded[..., :-2, :] - 6.0 * centre


def drift(padded, mob):
    centre = padded[..., 1:-1, :]
    return mob * (stiffness * laplace(padded) + centre - centre * centre * centre)


def general(path, start_image, end_image, labels, mob_table):
    count = path.shape[0]
    groups = lax.axis_size("img")
    images = count * groups
    rank = lax.axis_index("img")
    is_first = rank == 0
    is_final = rank == groups - 1
    gy_count = lax.axis_size("gy")
    rows_here = path.shape[2]
    cells = images * path.shape[1] * rows_here * gy_count * path.shape[3]
    mob = mobility(labels, mob_table)
    for step in range(ITERS):
        extended = jnp.concatenate([start_image[None], path], 0)
        padded = extended_2(extended, (("gy", 2),), 1)
        force = drift(padded, mob)
        current = padded[1 : count + 1, :, 1:-1, :]
        start_part = padded[0, :, 1:-1, :]
        ahead = shifted(current[0], "img", -1)
        ahead = jnp.where(is_final, end_image, ahead)
        later = jnp.concatenate([current[1:], ahead[None]], 0)
        wide_res = (later - current) / time_step - force[1:]
        opening = (current[0] - start_part) / time_step - force[0]
        mres = mob * wide_res
        mpad = extended_2(mres, (("gy", 2),), 1)
        previous = shifted(wide_res[-1], "img", 1)
        previous = jnp.where(is_first, opening, previous)
        earlier = jnp.concatenate([previous[None], wide_res[:-1]], 0)
        adjoint = stiffness * laplace(mpad) + (1.0 - 3.0 * path * path) * mres
        grad = (earlier - wide_res) / time_step - adjoint
        flat = grad.reshape(count, groups, -1)
        columns = lax.all_to_all(flat, "img", split_axis=1, concat_axis=0, tiled=True)
        every = columns.shape[0]
        index = jnp.arange(1, every + 1).astype(jnp.float32)[:, None, None]
        scaled = index * columns
        before_g = jnp.cumsum(columns, 0) - columns
        before_q = jnp.cumsum(scaled, 0) - scaled
        coeff = jnp.sum(columns, 0) - jnp.sum(scaled, 0) / (every + 1)
        solved = time_step * time_step * (index * coeff[None] - index * before_g + before_q)
        back = lax.all_to_all(solved, "img", split_axis=0, concat_axis=1, tiled=True)
        update = back.reshape(grad.shape)
        squares = lax.psum(jnp.sum(update * update), ("img", "gy"))
        scale = step_length * lax.rsqrt(squares / cells + 1e-06)
        path = path - scale * update
    return path


def walk(mesh):
    count = mesh.shape["img"]
    plain = list(range(count))
    try:
        line = mesh.devices.reshape(count, -1)[:, 0]
        place = [tuple(d.coords) for d in line]
    except Exception:
        return plain

    def near(a, b):
        return sum(abs(p - q) for p, q in zip(place[a], place[b])) <= 1

    def grow(order):
        if len(order) == count:
            return order
        for nxt in plain:
            if nxt not in order and near(order[-1], nxt):
                found = grow(order + [nxt])
                if found:
                    return found
        return None

    return grow([0]) or plain


def spread(order, position, flip):
    return jnp.where(flip == 1, order[len(order) - 1 - position], order[position])


def pack_kernel(order, path_ref, start_ref, end_ref, labels_ref, table_ref, out_ref):
    images, planes, rows, lanes = path_ref.shape
    groups = len(order)
    flip = lax.rem(lax.axis_index("gy"), 2)
    rank = lax.axis_index("img")
    slab = rank // 2
    odd = lax.rem(rank, 2) == 1
    for c in range(groups):
        dest = spread(order, c, flip)
        for m in range(images):
            for h in range(2):
                row = 4 * c + 2 * h
                parts = [path_ref[m, x, row : row + 2, :] for x in range(planes)]
                out_ref[dest, 2 * m + h] = jnp.concatenate(parts, 0)
        extra = []
        for h in range(2):
            row = 4 * c + 2 * h

            def tile(ref):
                parts = [ref[x, row : row + 2, :] for x in range(planes)]
                return jnp.concatenate(parts, 0)

            label = tile(labels_ref)
            mob = jnp.zeros(label.shape, jnp.float32)
            for level in range(table_ref.shape[0]):
                mob = mob + jnp.where(label == level, table_ref[level], jnp.float32(0.0))
            ends = jnp.where(slab == 0, tile(start_ref), tile(end_ref))
            extra.append(jnp.where(slab >= 2, mob, ends))
        out_ref[dest, 2 * images] = jnp.where(odd, extra[1], extra[0])


def lap(tiles):
    sublanes, lanes = tiles[0].shape
    r_is_0 = lax.rem(lax.broadcasted_iota(jnp.int32, tiles[0].shape, 0), 2) == 0
    out = []
    pair = [tiles[h] + tiles[h + 1] for h in range(len(tiles) - 1)]
    for h in range(1, len(tiles) - 1):
        v = tiles[h]
        total = pltpu.roll(v, 2, 0) + pltpu.roll(v, sublanes - 2, 0)
        total = total + pltpu.roll(v, 1, 1) + pltpu.roll(v, lanes - 1, 1)
        lower, upper = pltpu.roll(pair[h - 1], sublanes - 1, 0), pltpu.roll(pair[h], 1, 0)
        out.append(total + jnp.where(r_is_0, lower, upper) - 6.0 * v)
    return out


def pad_zero(tiles):
    zero = jnp.zeros_like(tiles[0])
    return [zero] + list(tiles) + [zero]


def residual(now, ahead, mob):
    out = []
    for v, w, q, m in zip(now, ahead, lap(pad_zero(now)), mob):
        force = m * (stiffness * q + v - v * v * v)
        out.append((w - v) * (1.0 / time_step) - force)
    return out


def gradient(now, before, resid, mres):
    out = []
    for n, q in enumerate(lap(mres)):
        v = now[n + 1]
        adjoint = stiffness * q + (1.0 - 3.0 * v * v) * mres[n + 1]
        out.append((before[n] - resid[n + 1]) * (1.0 / time_step) - adjoint)
    return out


def fetch(refs, group, tile_at):
    out = []
    for ref in refs:
        out += [ref[group, tile_at], ref[group, tile_at + 1]]
    return out


def fetch_extra(refs, slab):
    last = refs[0].shape[1] - 1
    out = []
    for ref in refs:
        out += [ref[2 * slab, last], ref[2 * slab + 1, last]]
    return out


DEGREE = 5


def iterations_kernel(order, own_ref, prev_ref, next_ref, field_ref, part_ref, w_ref, mres_ref):
    refs = (prev_ref, own_ref, next_ref)
    groups, per = own_ref.shape[0], own_ref.shape[1] // 2
    count = groups * per
    shape = own_ref.shape[2:]
    zero = jnp.zeros(shape, jnp.float32)
    slope = 1.0 / time_step

    def first_group(i, carry, last_group):
        before, psum, w = carry
        mob = fetch_extra(refs, 2)
        for m in range(per):
            k = i * per + m
            now = fetch(refs, i, 2 * m)
            if m < per - 1:
                ahead = fetch(refs, i, 2 * m + 2)
            elif last_group:
                ahead = fetch_extra(refs, 1)
            else:
                ahead = fetch(refs, i + 1, 0)
            resid = residual(now, ahead, mob)
            mres = [a * b for a, b in zip(mob, resid)]
            grad = gradient(now, before, resid, mres)
            for t in range(4):
                w_ref[k, t] = w[t]
            for t in range(2):
                mres_ref[k, t] = mres[t + 2]
            psum = tuple(p + g for p, g in zip(psum, grad))
            w = tuple(a - p for a, p in zip(w, psum))
            before = tuple(resid[1:-1])
        return before, psum, w

    opening = residual(fetch_extra(refs, 0), fetch(refs, 0, 0), fetch_extra(refs, 2))
    carry = tuple(opening[1:-1]), (zero,) * 4, (zero,) * 4
    carry = lax.fori_loop(0, groups - 1, lambda i, c: first_group(i, c, False), carry)
    w = first_group(groups - 1, carry, True)[2]

    gy, rank = lax.axis_index("gy"), lax.axis_index("img")
    final = lax.axis_size("gy") - 1
    opens = (gy == 0) & (rank == order[0])
    closes = (gy == final) & (rank == (order[0] if final % 2 else order[-1]))
    whole = jnp.float32(time_step * time_step)
    none = jnp.float32(0.0)
    keep = [jnp.where(opens, none, whole), whole, whole, jnp.where(closes, none, whole)]
    share = [v * (1.0 / (count + 1)) for v in w]

    def update_group(i, peak):
        for m in range(per):
            k = i * per + m
            at = (k + 1).astype(jnp.float32)
            for t in range(4):
                u = keep[t] * (w_ref[k, t] - at * share[t])
                w_ref[k, t] = u
                peak = jnp.maximum(peak, jnp.abs(u))
                if t in (1, 2):
                    field_ref[k, t - 1] = u
        return peak

    peak = lax.fori_loop(0, groups, update_group, zero)
    for t in range(4):
        w_ref[count, t] = zero
    sigma = jnp.maximum(jnp.max(peak), jnp.float32(1e-30))
    inverse = 1.0 / sigma

    def second_group(i, carry):
        v, before, psum, w = carry
        mob = fetch_extra(refs, 2)[1:-1]
        for m in range(per):
            k = i * per + m
            path = fetch(refs, i, 2 * m)[1:-1]
            ahead = [w_ref[k + 1, t] * inverse for t in range(4)]
            r1, m1, m2, m3, r2, r3 = [], [], [], [], [], []
            for t, q in enumerate(lap(pad_zero(v))):
                a, b, p = v[t], mob[t], path[t]
                one = b * (stiffness * q + a - 3.0 * p * p * a) - slope * (ahead[t] - a)
                ba = b * a
                two = 3.0 * p * a * ba
                three = -a * a * ba
                r1.append(one)
                r2.append(two)
                r3.append(three)
                m1.append(b * one)
                m2.append(b * two)
                m3.append(b * three)
            l1, l2, l3 = lap(m1), lap(m2), lap(m3)
            grads, later = [], []
            for t in range(2):
                a, p, m0 = v[t + 1], path[t + 1], mres_ref[k, t]
                e0, e1, e2 = 1.0 - 3.0 * p * p, 6.0 * p * a, -3.0 * a * a
                n1, n2, n3 = m1[t + 1], m2[t + 1], m3[t + 1]
                s1, s2, s3 = r1[t + 1], r2[t + 1], r3[t + 1]
                b1, b2, b3 = before[t]
                grads.append((
                    slope * (b1 - s1) - stiffness * l1[t] - (e0 * n1 + e1 * m0),
                    slope * (b2 - s2) - stiffness * l2[t] - (e0 * n2 + e1 * n1 + e2 * m0),
                    slope * (b3 - s3) - stiffness * l3[t] - (e0 * n3 + e1 * n2 + e2 * n1),
                    -(e1 * n3 + e2 * n2),
                    -(e2 * n3),
                ))
                later.append((s1, s2, s3))
            for t in range(2):
                for n in range(DEGREE):
                    field_ref[k, 2 * n + 2 + t] = w[t][n]
            psum = tuple(tuple(p + g for p, g in zip(psum[t], grads[t])) for t in range(2))
            w = tuple(tuple(a - p for a, p in zip(w[t], psum[t])) for t in range(2))
            before = tuple(later)
            v = tuple(ahead)
        return v, before, psum, w

    v = tuple(w_ref[0, t] * inverse for t in range(4))
    before = tuple((-slope * v[t + 1], zero, zero) for t in range(2))
    carry = v, before, ((zero,) * DEGREE,) * 2, ((zero,) * DEGREE,) * 2
    w = lax.fori_loop(0, groups, second_group, carry)[3]
    share = [[a * (1.0 / (count + 1)) for a in w[t]] for t in range(2)]

    def square_group(i, total):
        total = list(total)
        for m in range(per):
            k = i * per + m
            at = (k + 1).astype(jnp.float32)
            for t in range(2):
                f = [field_ref[k, t]]
                for n in range(DEGREE):
                    u = whole * (field_ref[k, 2 * n + 2 + t] - at * share[t][n])
                    field_ref[k, 2 * n + 2 + t] = u
                    f.append(u)
                for n in range(2 * DEGREE + 1):
                    low = [(a, n - a) for a in range(DEGREE + 1) if a < n - a <= DEGREE]
                    if low:
                        cross = functools.reduce(lambda x, y: x + y, [f[a] * f[b] for a, b in low])
                        cross = cross + cross
                        if n % 2 == 0:
                            cross = cross + f[n // 2] * f[n // 2]
                    else:
                        cross = f[n // 2] * f[n // 2]
                    total[n] = total[n] + cross
        return tuple(total)

    total = lax.fori_loop(0, groups, square_group, (zero,) * (2 * DEGREE + 1))
    rows = [jnp.sum(v, axis=0, keepdims=True) for v in total]
    rows += [jnp.zeros_like(rows[0])] * (16 - len(rows))
    sums = jnp.sum(jnp.concatenate(rows, 0), axis=1, keepdims=True)
    where_to = lax.broadcasted_iota(jnp.int32, (16, shape[1]), 0)
    lane = lax.broadcasted_iota(jnp.int32, (16, shape[1]), 1)
    line = jnp.sum(jnp.where(lane == where_to, sums, 0.0), axis=0, keepdims=True)
    line = jnp.where(lane[:1] == 2 * DEGREE + 1, sigma, line)
    part_ref[...] = jnp.broadcast_to(line, part_ref.shape)


def last_kernel(cells, own_ref, field_ref, part_ref, parts_ref, out_ref):
    groups, per = out_ref.shape[0], out_ref.shape[1] // 2
    parts = parts_ref[...]
    lane = lax.broadcasted_iota(jnp.int32, parts.shape, 1)
    zero = jnp.float32(0.0)
    at_sigma = 2 * DEGREE + 1

    def scale_of(squares):
        return step_length * lax.rsqrt(squares / cells + 1e-06)

    first = scale_of(jnp.sum(jnp.where(lane == 0, parts, zero)))
    sigmas = jnp.sum(jnp.where(lane == at_sigma, parts, zero), axis=1, keepdims=True)
    power = jnp.broadcast_to(first * sigmas, parts.shape)
    terms = jnp.where(lane < at_sigma, parts, zero)
    for bit in range(4):
        terms = jnp.where((lane >> bit) & 1 == 1, terms * power, terms)
        power = power * power
    second = scale_of(jnp.maximum(jnp.sum(terms), zero))
    mine = part_ref[:1, :]
    x = first * jnp.sum(jnp.where(lane[:1] == at_sigma, mine, zero))
    for i in range(groups):
        for m in range(per):
            k = i * per + m
            for t in range(2):
                u = field_ref[k, t]
                total = field_ref[k, 2 * DEGREE + t]
                for n in range(DEGREE - 1, -1, -1):
                    total = total * x + field_ref[k, 2 * n + t]
                out_ref[i, 2 * m + t] = own_ref[i, 2 * m + t] - first * u - second * total


def unpack_kernel(order, data_ref, out_ref):
    images, planes, rows, lanes = out_ref.shape
    groups = len(order)
    flip = lax.rem(lax.axis_index("gy"), 2)
    for c in range(groups):
        src = spread(order, c, flip)
        for m in range(images):
            for h in range(2):
                row = 4 * c + 2 * h
                v = data_ref[src, 2 * m + h]
                for x in range(planes):
                    out_ref[m, x, row : row + 2, :] = v[2 * x : 2 * x + 2, :]


VMEM_LIMIT = 16 * 1024 * 1024
WHOLE_VMEM = 67043328


def call(kernel, outs, count, scalars=0, scratch=(), limit=VMEM_LIMIT):
    shapes = [jax.ShapeDtypeStruct(s, jnp.float32) for s in outs]
    places = [pl.BlockSpec(memory_space=pltpu.VMEM) for _ in outs]
    single = len(outs) == 1
    return pl.pallas_call(
        kernel,
        out_shape=shapes[0] if single else shapes,
        in_specs=[pl.BlockSpec(memory_space=pltpu.VMEM)] * count
        + [pl.BlockSpec(memory_space=pltpu.SMEM)] * scalars,
        out_specs=places[0] if single else places,
        scratch_shapes=[pltpu.VMEM(shape, jnp.float32) for shape in scratch],
        compiler_params=pltpu.CompilerParams(vmem_limit_bytes=limit),
    )


def blocked(order, path, start_image, end_image, labels, mob_table):
    images, planes, rows, lanes = path.shape
    groups, slabs = lax.axis_size("img"), lax.axis_size("gy")
    both = ("img", "gy")
    every = groups * slabs
    tile = (2 * planes, lanes)
    cells = images * groups * planes * rows * slabs * lanes
    line = []
    for g in range(slabs):
        line += [i * slabs + g for i in (order[::-1] if g % 2 else order)]
    ahead = [(line[n], line[n + 1]) for n in range(every - 1)]
    back = [(b, a) for a, b in ahead]

    def swap(v, axis):
        return lax.all_to_all(v, axis, split_axis=0, concat_axis=0, tiled=True)

    packed = call(
        functools.partial(pack_kernel, order),
        [(groups, 2 * images + 1) + tile],
        4,
        scalars=1,
        limit=WHOLE_VMEM,
    )(path, start_image, end_image, labels, mob_table)
    own = swap(packed, "img")
    prev = lax.ppermute(own, both, ahead)
    after = lax.ppermute(own, both, back)
    field, part = call(
        functools.partial(iterations_kernel, order),
        [(images * groups, 2 * DEGREE + 2) + tile, (every, lanes)],
        3,
        scratch=[(images * groups + 1, 4) + tile, (images * groups, 2) + tile],
    )(own, prev, after)
    parts = swap(part, both)
    done = call(functools.partial(last_kernel, cells), [(groups, 2 * images) + tile], 4)(
        own, field, part, parts
    )
    home = swap(done, "img")
    return call(functools.partial(unpack_kernel, order), [path.shape], 1)(home)


def solution(mesh):
    order = walk(mesh)

    def per_device(path, start_image, end_image, labels, mob_table):
        images, planes, rows, lanes = path.shape
        groups = lax.axis_size("img")
        fits = rows == 4 * groups and planes == 4 and lanes == 128 and groups >= 6
        if fits and ITERS == 2:
            return blocked(order, path, start_image, end_image, labels, mob_table)
        return general(path, start_image, end_image, labels, mob_table)

    in_specs = (
        P("img", None, "gy", None),
        P(None, "gy", None),
        P(None, "gy", None),
        P(None, "gy", None),
        P(),
    )
    out_specs = P("img", None, "gy", None)
    return jax.shard_map(
        per_device, mesh=mesh, in_specs=in_specs, out_specs=out_specs, check_vma=False
    )
```

```python
import functools

import jax
import jax.numpy as jnp
from jax import lax
from jax.experimental import pallas as pl
from jax.experimental.pallas import tpu as pltpu
from jax.sharding import PartitionSpec as P

ITERS = 2


time_step = 0.5
stiffness = 0.25
step_length = 0.05


def extended_2(shard, sides, width):
    for axis, dim in sides:
        size, length = (lax.axis_size(axis), shard.shape[dim])
        up = [(i, (i + 1) % size) for i in range(size - 1)]
        down = [(j, i) for i, j in up]
        last = lax.slice_in_dim(shard, length - width, length, axis=dim)
        initial = lax.slice_in_dim(shard, 0, width, axis=dim)
        before = lax.ppermute(last, axis, up)
        after = lax.ppermute(initial, axis, down)
        shard = jnp.concatenate([before, shard, after], axis=dim)
    return shard


def shifted(block, axis, distance):
    devices = range(lax.axis_size(axis))
    route = [(i - distance, i) for i in devices if i - distance in devices]
    return lax.ppermute(block, axis, route)


def mobility(labels, table):
    result = jnp.zeros(labels.shape, jnp.float32)
    for level in range(table.shape[0]):
        result = result + jnp.where(labels == level, table[level], jnp.float32(0.0))
    return result


def laplace(padded):
    centre = padded[..., 1:-1, :]
    total = jnp.roll(centre, 1, -3) + jnp.roll(centre, -1, -3)
    total = total + jnp.roll(centre, 1, -1) + jnp.roll(centre, -1, -1)
    return total + padded[..., 2:, :] + padded[..., :-2, :] - 6.0 * centre


def drift(padded, mob):
    centre = padded[..., 1:-1, :]
    return mob * (stiffness * laplace(padded) + centre - centre * centre * centre)


def general(path, start_image, end_image, labels, mob_table):
    count = path.shape[0]
    groups = lax.axis_size("img")
    images = count * groups
    rank = lax.axis_index("img")
    is_first = rank == 0
    is_final = rank == groups - 1
    gy_count = lax.axis_size("gy")
    rows_here = path.shape[2]
    cells = images * path.shape[1] * rows_here * gy_count * path.shape[3]
    mob = mobility(labels, mob_table)
    for step in range(ITERS):
        extended = jnp.concatenate([start_image[None], path], 0)
        padded = extended_2(extended, (("gy", 2),), 1)
        force = drift(padded, mob)
        current = padded[1 : count + 1, :, 1:-1, :]
        start_part = padded[0, :, 1:-1, :]
        ahead = shifted(current[0], "img", -1)
        ahead = jnp.where(is_final, end_image, ahead)
        later = jnp.concatenate([current[1:], ahead[None]], 0)
        wide_res = (later - current) / time_step - force[1:]
        opening = (current[0] - start_part) / time_step - force[0]
        mres = mob * wide_res
        mpad = extended_2(mres, (("gy", 2),), 1)
        previous = shifted(wide_res[-1], "img", 1)
        previous = jnp.where(is_first, opening, previous)
        earlier = jnp.concatenate([previous[None], wide_res[:-1]], 0)
        adjoint = stiffness * laplace(mpad) + (1.0 - 3.0 * path * path) * mres
        grad = (earlier - wide_res) / time_step - adjoint
        flat = grad.reshape(count, groups, -1)
        columns = lax.all_to_all(flat, "img", split_axis=1, concat_axis=0, tiled=True)
        every = columns.shape[0]
        index = jnp.arange(1, every + 1).astype(jnp.float32)[:, None, None]
        scaled = index * columns
        before_g = jnp.cumsum(columns, 0) - columns
        before_q = jnp.cumsum(scaled, 0) - scaled
        coeff = jnp.sum(columns, 0) - jnp.sum(scaled, 0) / (every + 1)
        solved = time_step * time_step * (index * coeff[None] - index * before_g + before_q)
        back = lax.all_to_all(solved, "img", split_axis=0, concat_axis=1, tiled=True)
        update = back.reshape(grad.shape)
        squares = lax.psum(jnp.sum(update * update), ("img", "gy"))
        scale = step_length * lax.rsqrt(squares / cells + 1e-06)
        path = path - scale * update
    return path


def walks(mesh):
    count, slabs = mesh.shape["img"], mesh.shape["gy"]
    plain = list(range(count))
    plan = [plain if g % 2 == 0 else plain[::-1] for g in range(slabs)]
    try:
        line = mesh.devices.reshape(count, -1)[:, 0]
        place = [tuple(d.coords) for d in line]
    except Exception:
        return plan

    def step(a, b):
        moved = [n for n, (p, q) in enumerate(zip(place[a], place[b])) if p != q]
        near = sum(abs(p - q) for p, q in zip(place[a], place[b])) <= 1
        return (moved[0] if moved else -1) if near else None

    def grow(order, sign):
        if len(order) == count:
            return order
        options = [n for n in plain if n not in order and step(order[-1], n) is not None]
        for nxt in sorted(options, key=lambda n: sign * step(order[-1], n)):
            found = grow(order + [nxt], sign)
            if found:
                return found
        return None

    found, start = [], 0
    for g in range(slabs):
        order = grow([start], 1 if g % 2 == 0 else -1)
        if not order:
            return plan
        found.append(order)
        start = order[-1]
    return found


def picked(options, index):
    out = jnp.asarray(options[0], jnp.int32)
    for n, v in enumerate(options[1:], 1):
        out = jnp.where(index == n, jnp.asarray(v, jnp.int32), out)
    return out


def holder(orders, position):
    return picked([order[position] for order in orders], lax.axis_index("gy"))


def block_here(orders):
    rank, gy = lax.axis_index("img"), lax.axis_index("gy")
    inverse = [[order.index(n) for n in range(len(order))] for order in orders]
    return picked([picked(places, rank) for places in inverse], gy)


def pack_kernel(orders, path_ref, start_ref, end_ref, labels_ref, table_ref, out_ref):
    images, planes, rows, lanes = path_ref.shape
    groups = len(orders[0])
    rank = lax.axis_index("img")
    slab = rank // 2
    odd = lax.rem(rank, 2) == 1
    slabs = []
    for x in range(planes):
        label = labels_ref[x]
        mob = jnp.zeros(label.shape, jnp.float32)
        for level in range(table_ref.shape[0]):
            mob = mob + jnp.where(label == level, table_ref[level], jnp.float32(0.0))
        ends = jnp.where(slab == 0, start_ref[x], end_ref[x])
        slabs.append(jnp.where(slab >= 2, mob, ends))
    for c in range(groups):
        dest = holder(orders, c)
        for m in range(images):
            for h in range(2):
                row = 4 * c + 2 * h
                parts = [path_ref[m, x, row : row + 2, :] for x in range(planes)]
                out_ref[dest, 2 * m + h] = jnp.concatenate(parts, 0)
        extra = []
        for h in range(2):
            row = 4 * c + 2 * h
            extra.append(jnp.concatenate([v[row : row + 2, :] for v in slabs], 0))
        out_ref[dest, 2 * images] = jnp.where(odd, extra[1], extra[0])


def around(tiles):
    sublanes, lanes = tiles[0].shape
    r_is_0 = lax.rem(lax.broadcasted_iota(jnp.int32, tiles[0].shape, 0), 2) == 0
    out = []
    pair = [tiles[h] + tiles[h + 1] for h in range(len(tiles) - 1)]
    for h in range(1, len(tiles) - 1):
        v = tiles[h]
        total = pltpu.roll(v, 2, 0) + pltpu.roll(v, sublanes - 2, 0)
        total = total + (pltpu.roll(v, 1, 1) + pltpu.roll(v, lanes - 1, 1))
        lower, upper = pltpu.roll(pair[h - 1], sublanes - 1, 0), pltpu.roll(pair[h], 1, 0)
        out.append(total + jnp.where(r_is_0, lower, upper))
    return out


def pad_zero(tiles):
    zero = jnp.zeros_like(tiles[0])
    return [zero] + list(tiles) + [zero]


FLAT = 6.0 - 1.0 / stiffness
BENT = 1.0 / stiffness


def residual(now, ahead, scaled):
    out = []
    for v, w, q, c in zip(now, ahead, around(pad_zero(now)), scaled):
        out.append((w - v) - c * (q - v * (FLAT + BENT * (v * v))))
    return out


def gradient(now, before, resid, mres):
    out = []
    for n, q in enumerate(around(mres)):
        v = now[n + 1]
        own = mres[n + 1] * (FLAT + 3.0 * BENT * (v * v))
        out.append((before[n] - resid[n + 1]) - (q - own))
    return out


def fetch(refs, group, tile_at):
    out = []
    for ref in refs:
        out += [ref[group, tile_at], ref[group, tile_at + 1]]
    return out


def fetch_extra(refs, slab):
    last = refs[0].shape[1] - 1
    out = []
    for ref in refs:
        out += [ref[2 * slab, last], ref[2 * slab + 1, last]]
    return out


DEGREE = 5


def iterations_kernel(
    orders, own_ref, prev_ref, next_ref, field_ref, part_ref, w_ref, mres_ref, scaled_ref
):
    refs = (prev_ref, own_ref, next_ref)
    groups, per = own_ref.shape[0], own_ref.shape[1] // 2
    count = groups * per
    shape = own_ref.shape[2:]
    zero = jnp.zeros(shape, jnp.float32)
    gy, block = lax.axis_index("gy"), block_here(orders)
    none, whole = jnp.float32(0.0), jnp.float32(1.0)
    lower = jnp.where((gy == 0) & (block == 0), none, whole)
    upper = jnp.where((gy == lax.axis_size("gy") - 1) & (block == groups - 1), none, whole)
    inside = [lower, lower, None, None, upper, upper]

    def masked(value, mask):
        return value if mask is None else mask * value

    for t, v in enumerate(fetch_extra(refs, 2)):
        scaled_ref[t] = masked((time_step * stiffness) * v, inside[t])

    def known(tiles):
        return [masked(v, inside[t]) if t in (1, 4) else v for t, v in enumerate(tiles)]

    def first_group(i, carry, last_group):
        before, psum, w = carry
        scaled = [scaled_ref[t] for t in range(6)]
        for m in range(per):
            k = i * per + m
            now = known(fetch(refs, i, 2 * m))
            if m < per - 1:
                ahead = fetch(refs, i, 2 * m + 2)
            elif last_group:
                ahead = fetch_extra(refs, 1)
            else:
                ahead = fetch(refs, i + 1, 0)
            resid = residual(now, ahead, scaled)
            mres = [a * b for a, b in zip(scaled, resid)]
            grad = gradient(now, before, resid, mres)
            for t in range(4):
                w_ref[k, t] = w[t]
            for t in range(2):
                mres_ref[k, t] = mres[t + 2]
            psum = tuple(p + g for p, g in zip(psum, grad))
            w = tuple(a - p for a, p in zip(w, psum))
            before = tuple(resid[1:-1])
        return before, psum, w

    scaled = [scaled_ref[t] for t in range(6)]
    opening = residual(known(fetch_extra(refs, 0)), fetch(refs, 0, 0), scaled)
    carry = tuple(opening[1:-1]), (zero,) * 4, (zero,) * 4
    carry = lax.fori_loop(0, groups - 1, lambda i, c: first_group(i, c, False), carry)
    w = first_group(groups - 1, carry, True)[2]

    share = [v * (1.0 / (count + 1)) for v in w]

    def update_group(i, peak):
        for m in range(per):
            k = i * per + m
            at = (k + 1).astype(jnp.float32)
            for t in range(4):
                u = masked(w_ref[k, t] - at * share[t], inside[t + 1])
                w_ref[k, t] = u
                peak = jnp.maximum(peak, jnp.abs(u))
                if t in (1, 2):
                    field_ref[k, t - 1] = u
        return peak

    peak = lax.fori_loop(0, groups, update_group, zero)
    for t in range(4):
        w_ref[count, t] = zero
    sigma = jnp.maximum(jnp.max(peak), jnp.float32(1e-30))
    inverse = 1.0 / sigma

    def second_group(i, carry):
        v, before, psum, w = carry
        scaled = [scaled_ref[t + 1] for t in range(4)]
        for m in range(per):
            k = i * per + m
            path = fetch(refs, i, 2 * m)[1:-1]
            ahead = [w_ref[k + 1, t] * inverse for t in range(4)]
            r1, r2, r3, m1, m2, m3 = [], [], [], [], [], []
            squares = []
            for t, q in enumerate(around(pad_zero(v))):
                a, c, p = v[t], scaled[t], path[t]
                pull = FLAT + 3.0 * BENT * (p * p)
                ca = c * a
                cross = (3.0 * BENT) * (p * a)
                bend = BENT * (a * a)
                one = c * (q - a * pull) - (ahead[t] - a)
                two = cross * ca
                three = bend * ca
                r1.append(one)
                r2.append(two)
                r3.append(three)
                m1.append(c * one)
                m2.append(c * two)
                m3.append(c * three)
                squares.append((pull, cross + cross, 3.0 * bend))
            q1, q2, q3 = around(m1), around(m2), around(m3)
            grads, later = [], []
            for t in range(2):
                pull, cross, bend = squares[t + 1]
                m0 = mres_ref[k, t]
                n1, n2, n3 = m1[t + 1], m2[t + 1], m3[t + 1]
                s1, s2, s3 = r1[t + 1], r2[t + 1], r3[t + 1]
                b1, b2, b3 = before[t]
                grads.append((
                    (b1 - s1) - (q1[t] - pull * n1) - cross * m0,
                    (b2 - s2) - (q2[t] - pull * n2) - (cross * n1 - bend * m0),
                    (s3 - b3) + (q3[t] - pull * n3) - (cross * n2 - bend * n1),
                    cross * n3 + bend * n2,
                    -(bend * n3),
                ))
                later.append((s1, s2, s3))
            for t in range(2):
                for n in range(DEGREE):
                    field_ref[k, 2 * n + 2 + t] = w[t][n]
            psum = tuple(tuple(p + g for p, g in zip(psum[t], grads[t])) for t in range(2))
            w = tuple(tuple(a - p for a, p in zip(w[t], psum[t])) for t in range(2))
            before = tuple(later)
            v = tuple(ahead)
        return v, before, psum, w

    v = tuple(w_ref[0, t] * inverse for t in range(4))
    before = tuple((-v[t + 1], zero, zero) for t in range(2))
    carry = v, before, ((zero,) * DEGREE,) * 2, ((zero,) * DEGREE,) * 2
    w = lax.fori_loop(0, groups, second_group, carry)[3]
    share = [[a * (1.0 / (count + 1)) for a in w[t]] for t in range(2)]

    def square_group(i, total):
        total = list(total)
        for m in range(per):
            k = i * per + m
            at = (k + 1).astype(jnp.float32)
            for t in range(2):
                f = [field_ref[k, t]]
                for n in range(DEGREE):
                    u = field_ref[k, 2 * n + 2 + t] - at * share[t][n]
                    field_ref[k, 2 * n + 2 + t] = u
                    f.append(u)
                for n in range(2 * DEGREE + 1):
                    low = [(a, n - a) for a in range(DEGREE + 1) if a < n - a <= DEGREE]
                    if low:
                        cross = functools.reduce(lambda x, y: x + y, [f[a] * f[b] for a, b in low])
                        cross = cross + cross
                        if n % 2 == 0:
                            cross = cross + f[n // 2] * f[n // 2]
                    else:
                        cross = f[n // 2] * f[n // 2]
                    total[n] = total[n] + cross
        return tuple(total)

    total = lax.fori_loop(0, groups, square_group, (zero,) * (2 * DEGREE + 1))
    rows = [jnp.sum(v, axis=0, keepdims=True) for v in total]
    rows += [jnp.zeros_like(rows[0])] * (16 - len(rows))
    sums = jnp.sum(jnp.concatenate(rows, 0), axis=1, keepdims=True)
    where_to = lax.broadcasted_iota(jnp.int32, (16, shape[1]), 0)
    lane = lax.broadcasted_iota(jnp.int32, (16, shape[1]), 1)
    line = jnp.sum(jnp.where(lane == where_to, sums, 0.0), axis=0, keepdims=True)
    line = jnp.where(lane[:1] == 2 * DEGREE + 1, sigma, line)
    part_ref[...] = jnp.broadcast_to(line, part_ref.shape)


def last_kernel(cells, own_ref, field_ref, part_ref, parts_ref, out_ref):
    groups, per = out_ref.shape[0], out_ref.shape[1] // 2
    parts = parts_ref[...]
    lane = lax.broadcasted_iota(jnp.int32, parts.shape, 1)
    zero = jnp.float32(0.0)
    at_sigma = 2 * DEGREE + 1

    def scale_of(squares):
        return step_length * lax.rsqrt(squares / cells + 1e-06)

    first = scale_of(jnp.sum(jnp.where(lane == 0, parts, zero)))
    sigmas = jnp.sum(jnp.where(lane == at_sigma, parts, zero), axis=1, keepdims=True)
    power = jnp.broadcast_to(first * sigmas, parts.shape)
    terms = jnp.where(lane < at_sigma, parts, zero)
    for bit in range(4):
        terms = jnp.where((lane >> bit) & 1 == 1, terms * power, terms)
        power = power * power
    second = scale_of(jnp.maximum(jnp.sum(terms), zero))
    mine = part_ref[:1, :]
    x = first * jnp.sum(jnp.where(lane[:1] == at_sigma, mine, zero))
    for i in range(groups):
        for m in range(per):
            k = i * per + m
            for t in range(2):
                u = field_ref[k, t]
                total = field_ref[k, 2 * DEGREE + t]
                for n in range(DEGREE - 1, -1, -1):
                    total = total * x + field_ref[k, 2 * n + t]
                out_ref[i, 2 * m + t] = own_ref[i, 2 * m + t] - first * u - second * total


def unpack_kernel(orders, data_ref, out_ref):
    images, planes, rows, lanes = out_ref.shape
    groups = len(orders[0])
    for c in range(groups):
        src = holder(orders, c)
        for m in range(images):
            for h in range(2):
                row = 4 * c + 2 * h
                v = data_ref[src, 2 * m + h]
                for x in range(planes):
                    out_ref[m, x, row : row + 2, :] = v[2 * x : 2 * x + 2, :]


VMEM_LIMIT = 16 * 1024 * 1024
WHOLE_VMEM = 67043328


def call(kernel, outs, count, scalars=0, scratch=(), limit=VMEM_LIMIT):
    shapes = [jax.ShapeDtypeStruct(s, jnp.float32) for s in outs]
    places = [pl.BlockSpec(memory_space=pltpu.VMEM) for _ in outs]
    single = len(outs) == 1
    return pl.pallas_call(
        kernel,
        out_shape=shapes[0] if single else shapes,
        in_specs=[pl.BlockSpec(memory_space=pltpu.VMEM)] * count
        + [pl.BlockSpec(memory_space=pltpu.SMEM)] * scalars,
        out_specs=places[0] if single else places,
        scratch_shapes=[pltpu.VMEM(shape, jnp.float32) for shape in scratch],
        compiler_params=pltpu.CompilerParams(vmem_limit_bytes=limit),
    )


def blocked(orders, path, start_image, end_image, labels, mob_table):
    images, planes, rows, lanes = path.shape
    groups, slabs = lax.axis_size("img"), lax.axis_size("gy")
    both = ("img", "gy")
    every = groups * slabs
    tile = (2 * planes, lanes)
    cells = images * groups * planes * rows * slabs * lanes
    line = [i * slabs + g for g in range(slabs) for i in orders[g]]
    ahead = [(line[n - 1], line[n]) for n in range(every)]
    back = [(b, a) for a, b in ahead]

    def swap(v, axis):
        return lax.all_to_all(v, axis, split_axis=0, concat_axis=0, tiled=True)

    packed = call(
        functools.partial(pack_kernel, orders),
        [(groups, 2 * images + 1) + tile],
        4,
        scalars=1,
        limit=WHOLE_VMEM,
    )(path, start_image, end_image, labels, mob_table)
    own = swap(packed, "img")
    prev = lax.ppermute(own, both, ahead)
    after = lax.ppermute(own, both, back)
    field, part = call(
        functools.partial(iterations_kernel, orders),
        [(images * groups, 2 * DEGREE + 2) + tile, (every, lanes)],
        3,
        scratch=[
            (images * groups + 1, 4) + tile,
            (images * groups, 2) + tile,
            (6,) + tile,
        ],
    )(own, prev, after)
    parts = swap(part, both)
    done = call(functools.partial(last_kernel, cells), [(groups, 2 * images) + tile], 4)(
        own, field, part, parts
    )
    home = swap(done, "img")
    return call(functools.partial(unpack_kernel, orders), [path.shape], 1)(home)


def solution(mesh):
    orders = walks(mesh)

    def per_device(path, start_image, end_image, labels, mob_table):
        images, planes, rows, lanes = path.shape
        groups = lax.axis_size("img")
        fits = rows == 4 * groups and planes == 4 and lanes == 128 and groups >= 6
        if fits and ITERS == 2:
            return blocked(orders, path, start_image, end_image, labels, mob_table)
        return general(path, start_image, end_image, labels, mob_table)

    in_specs = (
        P("img", None, "gy", None),
        P(None, "gy", None),
        P(None, "gy", None),
        P(None, "gy", None),
        P(),
    )
    out_specs = P("img", None, "gy", None)
    return jax.shard_map(
        per_device, mesh=mesh, in_specs=in_specs, out_specs=out_specs, check_vma=False
    )
```

```python
import functools

import jax
import jax.numpy as jnp
from jax import lax
from jax.experimental import pallas as pl
from jax.experimental.pallas import tpu as pltpu
from jax.sharding import PartitionSpec as P

ITERS = 2


time_step = 0.5
stiffness = 0.25
step_length = 0.05


def extended_2(shard, sides, width):
    for axis, dim in sides:
        size, length = (lax.axis_size(axis), shard.shape[dim])
        up = [(i, (i + 1) % size) for i in range(size - 1)]
        down = [(j, i) for i, j in up]
        last = lax.slice_in_dim(shard, length - width, length, axis=dim)
        initial = lax.slice_in_dim(shard, 0, width, axis=dim)
        before = lax.ppermute(last, axis, up)
        after = lax.ppermute(initial, axis, down)
        shard = jnp.concatenate([before, shard, after], axis=dim)
    return shard


def shifted(block, axis, distance):
    devices = range(lax.axis_size(axis))
    route = [(i - distance, i) for i in devices if i - distance in devices]
    return lax.ppermute(block, axis, route)


def mobility(labels, table):
    result = jnp.zeros(labels.shape, jnp.float32)
    for level in range(table.shape[0]):
        result = result + jnp.where(labels == level, table[level], jnp.float32(0.0))
    return result


def laplace(padded):
    centre = padded[..., 1:-1, :]
    total = jnp.roll(centre, 1, -3) + jnp.roll(centre, -1, -3)
    total = total + jnp.roll(centre, 1, -1) + jnp.roll(centre, -1, -1)
    return total + padded[..., 2:, :] + padded[..., :-2, :] - 6.0 * centre


def drift(padded, mob):
    centre = padded[..., 1:-1, :]
    return mob * (stiffness * laplace(padded) + centre - centre * centre * centre)


def general(path, start_image, end_image, labels, mob_table):
    count = path.shape[0]
    groups = lax.axis_size("img")
    images = count * groups
    rank = lax.axis_index("img")
    is_first = rank == 0
    is_final = rank == groups - 1
    gy_count = lax.axis_size("gy")
    rows_here = path.shape[2]
    cells = images * path.shape[1] * rows_here * gy_count * path.shape[3]
    mob = mobility(labels, mob_table)
    for step in range(ITERS):
        extended = jnp.concatenate([start_image[None], path], 0)
        padded = extended_2(extended, (("gy", 2),), 1)
        force = drift(padded, mob)
        current = padded[1 : count + 1, :, 1:-1, :]
        start_part = padded[0, :, 1:-1, :]
        ahead = shifted(current[0], "img", -1)
        ahead = jnp.where(is_final, end_image, ahead)
        later = jnp.concatenate([current[1:], ahead[None]], 0)
        wide_res = (later - current) / time_step - force[1:]
        opening = (current[0] - start_part) / time_step - force[0]
        mres = mob * wide_res
        mpad = extended_2(mres, (("gy", 2),), 1)
        previous = shifted(wide_res[-1], "img", 1)
        previous = jnp.where(is_first, opening, previous)
        earlier = jnp.concatenate([previous[None], wide_res[:-1]], 0)
        adjoint = stiffness * laplace(mpad) + (1.0 - 3.0 * path * path) * mres
        grad = (earlier - wide_res) / time_step - adjoint
        flat = grad.reshape(count, groups, -1)
        columns = lax.all_to_all(flat, "img", split_axis=1, concat_axis=0, tiled=True)
        every = columns.shape[0]
        index = jnp.arange(1, every + 1).astype(jnp.float32)[:, None, None]
        scaled = index * columns
        before_g = jnp.cumsum(columns, 0) - columns
        before_q = jnp.cumsum(scaled, 0) - scaled
        coeff = jnp.sum(columns, 0) - jnp.sum(scaled, 0) / (every + 1)
        solved = time_step * time_step * (index * coeff[None] - index * before_g + before_q)
        back = lax.all_to_all(solved, "img", split_axis=0, concat_axis=1, tiled=True)
        update = back.reshape(grad.shape)
        squares = lax.psum(jnp.sum(update * update), ("img", "gy"))
        scale = step_length * lax.rsqrt(squares / cells + 1e-06)
        path = path - scale * update
    return path


def walks(mesh):
    count, slabs = mesh.shape["img"], mesh.shape["gy"]
    plain = list(range(count))
    plan = [plain if g % 2 == 0 else plain[::-1] for g in range(slabs)]
    try:
        line = mesh.devices.reshape(count, -1)[:, 0]
        place = [tuple(d.coords) for d in line]
    except Exception:
        return plan

    def step(a, b):
        moved = [n for n, (p, q) in enumerate(zip(place[a], place[b])) if p != q]
        near = sum(abs(p - q) for p, q in zip(place[a], place[b])) <= 1
        return (moved[0] if moved else -1) if near else None

    def grow(order, sign):
        if len(order) == count:
            return order
        options = [n for n in plain if n not in order and step(order[-1], n) is not None]
        for nxt in sorted(options, key=lambda n: sign * step(order[-1], n)):
            found = grow(order + [nxt], sign)
            if found:
                return found
        return None

    found, start = [], 0
    for g in range(slabs):
        order = grow([start], 1 if g % 2 == 0 else -1)
        if not order:
            return plan
        found.append(order)
        start = order[-1]
    return found


def picked(options, index):
    out = jnp.asarray(options[0], jnp.int32)
    for n, v in enumerate(options[1:], 1):
        out = jnp.where(index == n, jnp.asarray(v, jnp.int32), out)
    return out


def holder(orders, position):
    return picked([order[position] for order in orders], lax.axis_index("gy"))


def block_here(orders):
    rank, gy = lax.axis_index("img"), lax.axis_index("gy")
    inverse = [[order.index(n) for n in range(len(order))] for order in orders]
    return picked([picked(places, rank) for places in inverse], gy)


def pack_kernel(orders, path_ref, start_ref, end_ref, labels_ref, table_ref, out_ref, fixed_ref):
    images, planes, rows, lanes = path_ref.shape
    block = block_here(orders)
    for c in range(len(orders[0])):
        dest = holder(orders, c)

        def tile(ref, h, *at):
            row = 4 * c + 2 * h
            parts = [ref[at + (x, slice(row, row + 2))] for x in range(planes)]
            return jnp.concatenate(parts, 0)

        for m in range(images):
            for h in range(2):
                out_ref[dest, 2 * m + h] = tile(path_ref, h, m)

        @pl.when(block == c)
        def _():
            for h in range(2):
                label = tile(labels_ref, h)
                mob = jnp.zeros(label.shape, jnp.float32)
                for level in range(table_ref.shape[0]):
                    mob = mob + jnp.where(label == level, table_ref[level], jnp.float32(0.0))
                for slab, value in enumerate((tile(start_ref, h), tile(end_ref, h), mob)):
                    fixed_ref[2 * slab + h] = value


def around(tiles):
    sublanes, lanes = tiles[0].shape
    r_is_0 = lax.rem(lax.broadcasted_iota(jnp.int32, tiles[0].shape, 0), 2) == 0
    out = []
    pair = [tiles[h] + tiles[h + 1] for h in range(len(tiles) - 1)]
    for h in range(1, len(tiles) - 1):
        v = tiles[h]
        total = pltpu.roll(v, 2, 0) + pltpu.roll(v, sublanes - 2, 0)
        total = total + (pltpu.roll(v, 1, 1) + pltpu.roll(v, lanes - 1, 1))
        lower, upper = pltpu.roll(pair[h - 1], sublanes - 1, 0), pltpu.roll(pair[h], 1, 0)
        out.append(total + jnp.where(r_is_0, lower, upper))
    return out


def pad_zero(tiles):
    zero = jnp.zeros_like(tiles[0])
    return [zero] + list(tiles) + [zero]


FLAT = 6.0 - 1.0 / stiffness
BENT = 1.0 / stiffness


def residual(now, ahead, scaled):
    out = []
    for v, w, q, c in zip(now, ahead, around(pad_zero(now)), scaled):
        out.append((w - v) - c * (q - v * (FLAT + BENT * (v * v))))
    return out


def gradient(now, before, resid, mres):
    out = []
    for n, q in enumerate(around(mres)):
        v = now[n + 1]
        own = mres[n + 1] * (FLAT + 3.0 * BENT * (v * v))
        out.append((before[n] - resid[n + 1]) - (q - own))
    return out


def fetch(refs, group, tile_at):
    out = []
    for ref in refs:
        out += [ref[group, tile_at], ref[group, tile_at + 1]]
    return out


def fetch_fixed(refs, slab):
    before, own, after = refs
    last = own.shape[0] - 1
    out = [before[2 * slab], before[2 * slab + 1]]
    out += [own[last - 2 * slab], own[last - 2 * slab - 1]]
    return out + [after[2 * slab], after[2 * slab + 1]]


DEGREE = 5


def iterations_kernel(
    orders, own_ref, prev_ref, next_ref, fixed_ref, fixed_prev_ref, fixed_next_ref, field_ref, part_ref, w_ref, mres_ref, scaled_ref
):
    refs = (prev_ref, own_ref, next_ref)
    fixed = (fixed_prev_ref, fixed_ref, fixed_next_ref)
    groups, per = own_ref.shape[0], own_ref.shape[1] // 2
    count = groups * per
    shape = own_ref.shape[2:]
    zero = jnp.zeros(shape, jnp.float32)
    gy, block = lax.axis_index("gy"), block_here(orders)
    none, whole = jnp.float32(0.0), jnp.float32(1.0)
    lower = jnp.where((gy == 0) & (block == 0), none, whole)
    upper = jnp.where((gy == lax.axis_size("gy") - 1) & (block == groups - 1), none, whole)
    inside = [lower, lower, None, None, upper, upper]

    def masked(value, mask):
        return value if mask is None else mask * value

    for t, v in enumerate(fetch_fixed(fixed, 2)):
        scaled_ref[t] = masked((time_step * stiffness) * v, inside[t])

    def known(tiles):
        return [masked(v, inside[t]) if t in (1, 4) else v for t, v in enumerate(tiles)]

    def first_group(i, carry, last_group):
        before, psum, w = carry
        scaled = [scaled_ref[t] for t in range(6)]
        for m in range(per):
            k = i * per + m
            now = known(fetch(refs, i, 2 * m))
            if m < per - 1:
                ahead = fetch(refs, i, 2 * m + 2)
            elif last_group:
                ahead = fetch_fixed(fixed, 1)
            else:
                ahead = fetch(refs, i + 1, 0)
            resid = residual(now, ahead, scaled)
            mres = [a * b for a, b in zip(scaled, resid)]
            grad = gradient(now, before, resid, mres)
            for t in range(4):
                w_ref[k, t] = w[t]
            for t in range(2):
                mres_ref[k, t] = mres[t + 2]
            psum = tuple(p + g for p, g in zip(psum, grad))
            w = tuple(a - p for a, p in zip(w, psum))
            before = tuple(resid[1:-1])
        return before, psum, w

    scaled = [scaled_ref[t] for t in range(6)]
    opening = residual(known(fetch_fixed(fixed, 0)), fetch(refs, 0, 0), scaled)
    carry = tuple(opening[1:-1]), (zero,) * 4, (zero,) * 4
    carry = lax.fori_loop(0, groups - 1, lambda i, c: first_group(i, c, False), carry)
    w = first_group(groups - 1, carry, True)[2]

    share = [v * (1.0 / (count + 1)) for v in w]

    def update_group(i, peak):
        for m in range(per):
            k = i * per + m
            at = (k + 1).astype(jnp.float32)
            for t in range(4):
                u = masked(w_ref[k, t] - at * share[t], inside[t + 1])
                w_ref[k, t] = u
                peak = jnp.maximum(peak, jnp.abs(u))
                if t in (1, 2):
                    field_ref[k, t - 1] = u
        return peak

    peak = lax.fori_loop(0, groups, update_group, zero)
    for t in range(4):
        w_ref[count, t] = zero
    sigma = jnp.maximum(jnp.max(peak), jnp.float32(1e-30))
    inverse = 1.0 / sigma

    def second_group(i, carry):
        v, before, psum, w = carry
        scaled = [scaled_ref[t + 1] for t in range(4)]
        for m in range(per):
            k = i * per + m
            path = fetch(refs, i, 2 * m)[1:-1]
            ahead = [w_ref[k + 1, t] * inverse for t in range(4)]
            r1, r2, r3, m1, m2, m3 = [], [], [], [], [], []
            squares = []
            for t, q in enumerate(around(pad_zero(v))):
                a, c, p = v[t], scaled[t], path[t]
                pull = FLAT + 3.0 * BENT * (p * p)
                ca = c * a
                cross = (3.0 * BENT) * (p * a)
                bend = BENT * (a * a)
                one = c * (q - a * pull) - (ahead[t] - a)
                two = cross * ca
                three = bend * ca
                r1.append(one)
                r2.append(two)
                r3.append(three)
                m1.append(c * one)
                m2.append(c * two)
                m3.append(c * three)
                squares.append((pull, cross + cross, 3.0 * bend))
            q1, q2, q3 = around(m1), around(m2), around(m3)
            grads, later = [], []
            for t in range(2):
                pull, cross, bend = squares[t + 1]
                m0 = mres_ref[k, t]
                n1, n2, n3 = m1[t + 1], m2[t + 1], m3[t + 1]
                s1, s2, s3 = r1[t + 1], r2[t + 1], r3[t + 1]
                b1, b2, b3 = before[t]
                grads.append((
                    (b1 - s1) - (q1[t] - pull * n1) - cross * m0,
                    (b2 - s2) - (q2[t] - pull * n2) - (cross * n1 - bend * m0),
                    (s3 - b3) + (q3[t] - pull * n3) - (cross * n2 - bend * n1),
                    cross * n3 + bend * n2,
                    -(bend * n3),
                ))
                later.append((s1, s2, s3))
            for t in range(2):
                for n in range(DEGREE):
                    field_ref[k, 2 * n + 2 + t] = w[t][n]
            psum = tuple(tuple(p + g for p, g in zip(psum[t], grads[t])) for t in range(2))
            w = tuple(tuple(a - p for a, p in zip(w[t], psum[t])) for t in range(2))
            before = tuple(later)
            v = tuple(ahead)
        return v, before, psum, w

    v = tuple(w_ref[0, t] * inverse for t in range(4))
    before = tuple((-v[t + 1], zero, zero) for t in range(2))
    carry = v, before, ((zero,) * DEGREE,) * 2, ((zero,) * DEGREE,) * 2
    w = lax.fori_loop(0, groups, second_group, carry)[3]
    share = [[a * (1.0 / (count + 1)) for a in w[t]] for t in range(2)]

    def square_group(i, total):
        total = list(total)
        for m in range(per):
            k = i * per + m
            at = (k + 1).astype(jnp.float32)
            for t in range(2):
                f = [field_ref[k, t]]
                for n in range(DEGREE):
                    u = field_ref[k, 2 * n + 2 + t] - at * share[t][n]
                    field_ref[k, 2 * n + 2 + t] = u
                    f.append(u)
                for n in range(2 * DEGREE + 1):
                    low = [(a, n - a) for a in range(DEGREE + 1) if a < n - a <= DEGREE]
                    if low:
                        cross = functools.reduce(lambda x, y: x + y, [f[a] * f[b] for a, b in low])
                        cross = cross + cross
                        if n % 2 == 0:
                            cross = cross + f[n // 2] * f[n // 2]
                    else:
                        cross = f[n // 2] * f[n // 2]
                    total[n] = total[n] + cross
        return tuple(total)

    total = lax.fori_loop(0, groups, square_group, (zero,) * (2 * DEGREE + 1))
    rows = [jnp.sum(v, axis=0, keepdims=True) for v in total]
    rows += [jnp.zeros_like(rows[0])] * (16 - len(rows))
    sums = jnp.sum(jnp.concatenate(rows, 0), axis=1, keepdims=True)
    where_to = lax.broadcasted_iota(jnp.int32, (16, shape[1]), 0)
    lane = lax.broadcasted_iota(jnp.int32, (16, shape[1]), 1)
    line = jnp.sum(jnp.where(lane == where_to, sums, 0.0), axis=0, keepdims=True)
    line = jnp.where(lane[:1] == 2 * DEGREE + 1, sigma, line)
    part_ref[...] = jnp.broadcast_to(line, part_ref.shape)


def last_kernel(cells, own_ref, field_ref, part_ref, parts_ref, out_ref):
    groups, per = out_ref.shape[0], out_ref.shape[1] // 2
    parts = parts_ref[...]
    lane = lax.broadcasted_iota(jnp.int32, parts.shape, 1)
    zero = jnp.float32(0.0)
    at_sigma = 2 * DEGREE + 1

    def scale_of(squares):
        return step_length * lax.rsqrt(squares / cells + 1e-06)

    first = scale_of(jnp.sum(jnp.where(lane == 0, parts, zero)))
    sigmas = jnp.sum(jnp.where(lane == at_sigma, parts, zero), axis=1, keepdims=True)
    power = jnp.broadcast_to(first * sigmas, parts.shape)
    terms = jnp.where(lane < at_sigma, parts, zero)
    for bit in range(4):
        terms = jnp.where((lane >> bit) & 1 == 1, terms * power, terms)
        power = power * power
    second = scale_of(jnp.maximum(jnp.sum(terms), zero))
    mine = part_ref[:1, :]
    x = first * jnp.sum(jnp.where(lane[:1] == at_sigma, mine, zero))
    for i in range(groups):
        for m in range(per):
            k = i * per + m
            for t in range(2):
                u = field_ref[k, t]
                total = field_ref[k, 2 * DEGREE + t]
                for n in range(DEGREE - 1, -1, -1):
                    total = total * x + field_ref[k, 2 * n + t]
                out_ref[i, 2 * m + t] = own_ref[i, 2 * m + t] - first * u - second * total


def unpack_kernel(orders, data_ref, out_ref):
    images, planes, rows, lanes = out_ref.shape
    groups = len(orders[0])
    for c in range(groups):
        src = holder(orders, c)
        for m in range(images):
            for h in range(2):
                row = 4 * c + 2 * h
                v = data_ref[src, 2 * m + h]
                for x in range(planes):
                    out_ref[m, x, row : row + 2, :] = v[2 * x : 2 * x + 2, :]


VMEM_LIMIT = 16 * 1024 * 1024
WHOLE_VMEM = 67043328


def call(kernel, outs, count, scalars=0, scratch=(), limit=VMEM_LIMIT):
    shapes = [jax.ShapeDtypeStruct(s, jnp.float32) for s in outs]
    places = [pl.BlockSpec(memory_space=pltpu.VMEM) for _ in outs]
    single = len(outs) == 1
    return pl.pallas_call(
        kernel,
        out_shape=shapes[0] if single else shapes,
        in_specs=[pl.BlockSpec(memory_space=pltpu.VMEM)] * count
        + [pl.BlockSpec(memory_space=pltpu.SMEM)] * scalars,
        out_specs=places[0] if single else places,
        scratch_shapes=[pltpu.VMEM(shape, jnp.float32) for shape in scratch],
        compiler_params=pltpu.CompilerParams(vmem_limit_bytes=limit),
    )


def blocked(orders, path, start_image, end_image, labels, mob_table):
    images, planes, rows, lanes = path.shape
    groups, slabs = lax.axis_size("img"), lax.axis_size("gy")
    both = ("img", "gy")
    every = groups * slabs
    tile = (2 * planes, lanes)
    cells = images * groups * planes * rows * slabs * lanes
    line = [i * slabs + g for g in range(slabs) for i in orders[g]]
    ahead = [(line[n - 1], line[n]) for n in range(every)]
    back = [(b, a) for a, b in ahead]

    def swap(v, axis):
        return lax.all_to_all(v, axis, split_axis=0, concat_axis=0, tiled=True)

    packed, fixed = call(
        functools.partial(pack_kernel, orders),
        [(groups, 2 * images) + tile, (6,) + tile],
        4,
        scalars=1,
        limit=WHOLE_VMEM,
    )(path, start_image, end_image, labels, mob_table)
    own = swap(packed, "img")
    blocks = [own] + [lax.ppermute(own, both, way) for way in (ahead, back)]
    blocks += [fixed[::-1]] + [lax.ppermute(fixed, both, way) for way in (ahead, back)]
    field, part = call(
        functools.partial(iterations_kernel, orders),
        [(images * groups, 2 * DEGREE + 2) + tile, (every, lanes)],
        6,
        scratch=[
            (images * groups + 1, 4) + tile,
            (images * groups, 2) + tile,
            (6,) + tile,
        ],
    )(*blocks)
    parts = swap(part, both)
    done = call(functools.partial(last_kernel, cells), [(groups, 2 * images) + tile], 4)(
        own, field, part, parts
    )
    home = swap(done, "img")
    return call(functools.partial(unpack_kernel, orders), [path.shape], 1)(home)


def solution(mesh):
    orders = walks(mesh)

    def per_device(path, start_image, end_image, labels, mob_table):
        images, planes, rows, lanes = path.shape
        groups = lax.axis_size("img")
        fits = rows == 4 * groups and planes == 4 and lanes == 128 and groups >= 6
        if fits and ITERS == 2:
            return blocked(orders, path, start_image, end_image, labels, mob_table)
        return general(path, start_image, end_image, labels, mob_table)

    in_specs = (
        P("img", None, "gy", None),
        P(None, "gy", None),
        P(None, "gy", None),
        P(None, "gy", None),
        P(),
    )
    out_specs = P("img", None, "gy", None)
    return jax.shard_map(
        per_device, mesh=mesh, in_specs=in_specs, out_specs=out_specs, check_vma=False
    )
```
